256 devices in a mesh: seq: 64 (over x, z, core), tp: 4 (over y).
Axes of the slice: x: 4, y: 4, z: 8, core: 2. Of those that a mesh axis runs over, the one named last changes fastest.
Arguments:
- token_ids: int32 [65536], P('seq'), may hold values from 0 to 511
- embed_table: bfloat16 [512, 2048], P(None, 'tp'), may hold values from -6 to 6
- norm_gain: float32 [2048], replicated, may hold values from 0.1 to 1.9
- in_weight: bfloat16 [2048, 3, 2048], P('seq', None, 'tp'), may hold values from -0.125 to 0.125
- short_filter: float32 [7, 3, 2048], P(None, None, 'tp'), may hold values from -2.4 to 2.4
- long_filter: bfloat16 [128, 128], P('tp'), may hold values from -0.5390625 to 0.5390625
- long_skip: float32 [2048], P('tp'), may hold values from -3 to 3
- out_weight: bfloat16 [2048, 2048], P('tp', 'seq'), may hold values from -0.125 to 0.125
Outputs:
- mixed: bfloat16 [65536, 2048], P('seq', 'tp')
The draws below stay inside these ranges and needn't reach their ends.
All inputs are finite; a program needn't handle non-finite values.
Results may differ from the reference program's by a relative error of at most 0.012.
Values may be sent and summed in bfloat16 or wider, within the bound.
A program may use at most 64 MiB of HBM per device.

```python
import math
import jax
import jax.numpy as jnp
import numpy as np
from jax import lax

D = 2048
VOCAB = 512
GROUP = 16
TAPS = 128
SHORT = 7
TOKENS = 65536
GROUPS = 128
N_TP = 4


def plant(entries, rng, smallest, top_value):
    longest = entries.shape.index(max(entries.shape))
    spots = []
    for shift in (0, 1):
        where = [jax.random.randint(jax.random.fold_in(rng, axis), (), 0, length) for axis, length in enumerate(entries.shape)]
        where[longest] = (where[longest] + shift) % entries.shape[longest]
        spots.append(tuple(where))
    return entries.at[spots[0]].set(smallest).at[spots[1]].set(top_value)


def levels(own_key, extent, shards, least, high):
    loudness = 1.0
    for dim, shards_of in shards:
        heights = jax.random.uniform(jax.random.fold_in(jax.random.fold_in(own_key, 6), dim), (shards_of,), jnp.float32, least / len(shards), high / len(shards))
        loudness = loudness * jnp.repeat(jnp.exp(heights), extent[dim] // shards_of).reshape((-1,) + (1,) * (len(extent) - 1 - dim))
    return loudness


def cumulative_ranks(count, slope):
    portions = [(1 << 20) // math.isqrt(grade ** slope) + 1 for grade in range(1, count + 1)]
    width = 1 + sum(portions) // (1 << 30)
    return np.cumsum(np.array([max(1, weight // width) for weight in portions]))


def ranked_ids(own_key, extent, amount, skew):
    listing = cumulative_ranks(amount, skew)
    ticket = jax.random.randint(jax.random.fold_in(own_key, 1), extent, 0, int(listing[amount - 1]))
    grade = jnp.searchsorted(jnp.asarray(listing, jnp.int32), ticket, side="right")
    return jax.random.permutation(jax.random.fold_in(own_key, 2), amount)[grade].astype(jnp.int32)


def scatter_about(rng, dims, spread, bound, cuts=(), kind=jnp.bfloat16):
    result = spread * jax.random.normal(rng, dims, jnp.float32)
    if cuts:
        result = result * levels(rng, dims, cuts, -0.22, 0.18)
    return jnp.clip(result, -bound, bound).astype(kind)


def setup_inputs(seed: int = 0) -> dict:
    arg_keys = jax.random.split(jax.random.key(seed), 9)
    token_ids = plant(ranked_ids(arg_keys[0], (TOKENS,), VOCAB, 2), jax.random.fold_in(arg_keys[0], 3), 0, VOCAB - 1).astype(jnp.int32)
    embed_table = scatter_about(arg_keys[1], (VOCAB, D), 1.0, 6.0, ((1, 4),))
    norm_gain = jnp.clip(1.0 + 0.18 * jax.random.normal(arg_keys[2], (D,), jnp.float32), 0.1, 1.9)
    in_weight = scatter_about(arg_keys[3], (D, 3, D), D ** -0.5, 0.125, ((0, 64), (2, 4)))
    short_filter = scatter_about(arg_keys[4], (SHORT, 3, D), 0.4, 2.4, ((2, 4),), jnp.float32)
    long_filter = scatter_about(arg_keys[5], (GROUPS, TAPS), 0.09, 0.5390625, ((0, 4),))
    long_skip = scatter_about(arg_keys[6], (D,), 0.7, 3.0, ((0, 4),), jnp.float32)
    out_weight = scatter_about(arg_keys[7], (D, D), D ** -0.5, 0.125, ((0, 4), (1, 64)))
    return {"token_ids": token_ids, "embed_table": embed_table, "norm_gain": norm_gain, "in_weight": in_weight, "short_filter": short_filter, "long_filter": long_filter, "long_skip": long_skip, "out_weight": out_weight}


def reference(token_ids, embed_table, norm_gain, in_weight, short_filter, long_filter, long_skip, out_weight):
    embedded = embed_table[token_ids]
    widened = embedded.astype(jnp.float32)
    scaled = widened * lax.rsqrt(lax.optimization_barrier(jnp.mean(widened * widened, axis=1, keepdims=True)) + 1e-06) * norm_gain[None, :]
    normed = scaled.astype(jnp.bfloat16)
    tok_total = normed.shape[0]
    projected = jnp.dot(normed, in_weight.reshape(D, 3 * D), preferred_element_type=jnp.float32)
    projected = projected.astype(jnp.bfloat16).reshape(tok_total, 3, D)
    padded = jnp.pad(projected, ((SHORT - 1, 0), (0, 0), (0, 0)))
    featured = jnp.zeros((tok_total, 3, D), jnp.float32)
    for tap_index in range(SHORT):
        begin = SHORT - 1 - tap_index
        featured = featured + short_filter[tap_index][None] * padded[begin:begin + tok_total].astype(jnp.float32)
    queries = featured[:, 0]
    product = (featured[:, 1] * featured[:, 2]).astype(jnp.bfloat16)
    taps_wide = jnp.repeat(long_filter.astype(jnp.float32), GROUP, axis=0)
    source = jnp.pad(product.astype(jnp.float32), ((TAPS - 1, 0), (0, 0)))

    def add_lag(tap_index, running):
        column = lax.dynamic_slice_in_dim(taps_wide, tap_index.astype(jnp.int32), 1, 1)[:, 0]
        begin = (TAPS - 1 - tap_index).astype(jnp.int32)
        return running + column[None, :] * lax.dynamic_slice_in_dim(source, begin, tok_total, 0)
    convolved = lax.fori_loop(0, TAPS, add_lag, jnp.zeros((tok_total, D), jnp.float32))
    convolved = convolved + long_skip[None, :] * product.astype(jnp.float32)
    gated = (queries * convolved).astype(jnp.bfloat16)
    band_width = D // N_TP
    running = jnp.zeros((tok_total, D), jnp.float32)
    for block_index in range(N_TP):
        lower = block_index * band_width
        partial_term = jnp.dot(gated[:, lower:lower + band_width], out_weight[lower:lower + band_width], preferred_element_type=jnp.float32).astype(jnp.bfloat16)
        partial_term = lax.optimization_barrier(partial_term)
        running = running + partial_term.astype(jnp.float32)
    return (widened + running).astype(jnp.bfloat16)
```

```python
import functools

import jax
import jax.numpy as jnp
from jax import lax
from jax.experimental import pallas as pl
from jax.experimental.pallas import tpu as pltpu
from jax.sharding import PartitionSpec as P

MESH = pl.DeviceIdType.MESH
BF16 = jnp.bfloat16
F32 = jnp.float32
NX, NZ, NC, NY = 4, 8, 2, 4
LINE = NZ * NC
TILES = 10


def kernel(
    tok_ref, emb_ref, gain_ref, w_ref, wo_ref, sf_ref, lf_ref, out_ref,
    tprev, sf2, lf2, wl, e4, tt, wt, g4, oneh, band, taps, proj, acc,
    tok_s, tok_r, fil_s, fil_r, s1_s, s1_r, s2_s, s2_r, e_s, e_r, wo_s, wo_r, t2_s, t2_r,
    ax_s, ax_r, az_s, az_r, ad_s, ad_r, g_s, g_r,
):
    s = lax.axis_index("seq")
    y = lax.axis_index("tp")
    zc = lax.rem(s, LINE)
    x = s // LINE
    z = zc // NC
    c = lax.rem(zc, NC)
    sign = 1 - 2 * c
    far = lax.rem(y + 2, NY)
    turned = y * LINE + zc

    def at_x(q):
        return (lax.rem(x + q, NX) * LINE + zc, y)

    def at_y(q):
        return (s, lax.rem(y + q, NY))

    def at_z(q):
        return (x * LINE + lax.rem(z + q + NZ, NZ) * NC + c, y)

    mate = (s + sign, y)
    after = (lax.rem(s + 1, NX * LINE), y)
    before = (lax.rem(s + NX * LINE - 1, NX * LINE), y)

    sent = []

    def copy(src, dst, ss, rs, dev):
        return pltpu.make_async_remote_copy(
            src_ref=src, dst_ref=dst, send_sem=ss, recv_sem=rs, device_id=dev, device_id_type=MESH
        )

    def send(*args):
        one = copy(*args)
        one.start()
        sent.append(one)

    hello = pltpu.get_barrier_semaphore()
    greeted = 0
    for r in range(1, LINE):
        pl.semaphore_signal(
            hello, inc=1, device_id=(x * LINE + lax.rem(zc + r, LINE), y), device_id_type=MESH
        )
        greeted += 1
    for r in range(1, NX):
        pl.semaphore_signal(hello, inc=1, device_id=at_x(r), device_id_type=MESH)
        pl.semaphore_signal(hello, inc=1, device_id=at_y(r), device_id_type=MESH)
        greeted += 2
    pl.semaphore_signal(hello, inc=1, device_id=after, device_id_type=MESH)
    pl.semaphore_signal(hello, inc=1, device_id=before, device_id_type=MESH)
    greeted += 2

    @pl.when(x != y)
    def _():
        pl.semaphore_signal(hello, inc=1, device_id=(turned, x), device_id_type=MESH)

    pl.semaphore_wait(hello, greeted + jnp.where(x == y, 0, 1))

    for r in range(1, LINE):
        other = lax.rem(zc + r, LINE)
        send(w_ref.at[other], wl.at[x, zc], s1_s.at[r - 1], s1_r.at[r - 1], (x * LINE + other, y))
    for r in range(1, NY):
        send(
            emb_ref.at[pl.ds(pl.multiple_of(x * 128, 128), 128)],
            e4.at[y], e_s.at[r - 1], e_r.at[r - 1], at_y(r),
        )
    send(tok_ref, tprev, tok_s, tok_r, after)
    send(sf_ref, sf2, fil_s.at[0], fil_r.at[0], at_y(2))
    send(lf_ref, lf2, fil_s.at[1], fil_r.at[1], at_y(2))

    @pl.when(x != y)
    def _():
        copy(wo_ref, wt.at[zc, y], wo_s, wo_r, (turned, x)).start()

    @pl.when(x == y)
    def _():
        wt[zc, x] = wo_ref[...]

    wl[x, zc] = w_ref[zc]
    e4[y] = emb_ref[pl.ds(pl.multiple_of(x * 128, 128), 128), :]

    ids = lax.broadcasted_iota(jnp.int32, (512, 128), 0)
    for tile in range(8):
        row = tok_ref[tile : tile + 1, :]
        oneh[:, (tile + 2) * 128 : (tile + 3) * 128] = (
            jnp.where(ids == row, 1.0, 0.0).astype(BF16)
        )

    above = lax.broadcasted_iota(jnp.int32, (128, 128), 1) >= lax.broadcasted_iota(
        jnp.int32, (128, 128), 0
    )

    def bands(which, filters):
        def build(g, carry):
            rows = jnp.broadcast_to(filters[pl.ds(g, 1), :], (128, 128))
            turnedrows = pltpu.roll(rows, 0, 1, stride=1, stride_axis=0)
            band[which, g, 0:128, :] = jnp.where(above, 0.0, turnedrows).astype(BF16)
            band[which, g, 128:256, :] = jnp.where(above, turnedrows, 0.0).astype(BF16)
            return carry

        lax.fori_loop(0, 32, build, 0)

    def columns(which, filters):
        for p in range(4):
            for part in range(3):
                taps[which, p, part] = filters[p, part].T

    columns(0, sf_ref)

    for r in range(1, LINE):
        copy(w_ref.at[0], wl.at[x, lax.rem(zc + LINE - r, LINE)], s1_s.at[r - 1], s1_r.at[r - 1], mate).wait_recv()
    for r in range(1, NX):
        send(wl.at[x], wl.at[x], s2_s.at[r - 1], s2_r.at[r - 1], at_x(r))
    for r in range(1, NY):
        copy(e4.at[0], e4.at[lax.rem(y + NY - r, NY)], e_s.at[r - 1], e_r.at[r - 1], mate).wait_recv()

    total = jnp.zeros((128, 1), F32)
    for k in range(NY):
        piece = e4[k].astype(F32)
        total = total + jnp.sum(piece * piece, axis=1, keepdims=True)
    scale = lax.rsqrt(total * (1.0 / 2048) + 1e-06)
    normed = [
        (e4[k].astype(F32) * scale * gain_ref[k]).astype(BF16) for k in range(NY)
    ]
    for r in range(1, NX):
        copy(wl.at[0], wl.at[lax.rem(x + NX - r, NX)], s2_s.at[r - 1], s2_r.at[r - 1], mate).wait_recv()
    table = jnp.zeros((128, 128), F32)
    for k in range(NX):
        table = table + jnp.dot(
            normed[k], wl[k].reshape(512, 128), preferred_element_type=F32
        )
    tt[0, zc, x] = table.T[0:96].astype(BF16)

    class Gather:
        def __init__(self, n, buf):
            self.n, self.buf = n, buf

        def xsend(self):
            for q in range(1, NX):
                here = self.buf.at[zc, x]
                send(here, here, ax_s.at[self.n, q - 1], ax_r.at[self.n, q - 1], at_x(q))

        def zsend(self, way, step, piece):
            hop = sign if way == 0 else -sign
            block = lax.rem(z - hop * (step - 1) + NZ, NZ) * NC + c
            here = self.buf.at[block, lax.rem(x + NX - piece, NX)]
            at = (self.n, way, step - 1, piece)
            send(here, here, az_s.at[at], az_r.at[at], at_z(hop))

        def zwait(self, way, step, piece):
            hop = sign if way == 0 else -sign
            block = lax.rem(z - hop * step + NZ, NZ) * NC + c
            here = self.buf.at[block, lax.rem(x + NX - piece, NX)]
            at = (self.n, way, step - 1, piece)
            copy(here, here, az_s.at[at], az_r.at[at], mate).wait_recv()
            return block

        def dsend(self, slot, block):
            here = self.buf.at[block]
            send(here, here, ad_s.at[self.n, slot], ad_r.at[self.n, slot], mate)

        def dwait(self, slot, block):
            here = self.buf.at[block]
            copy(here, here, ad_s.at[self.n, slot], ad_r.at[self.n, slot], mate).wait_recv()

        def first(self):
            self.xsend()
            for piece in range(NX):
                if piece:
                    there = self.buf.at[zc, lax.rem(x + NX - piece, NX)]
                    copy(there, there, ax_s.at[self.n, piece - 1], ax_r.at[self.n, piece - 1], mate).wait_recv()
                self.zsend(0, 1, piece)
                self.zsend(1, 1, piece)
            self.dsend(0, zc)

        def step(self, i):
            blocks = []
            for piece in range(NX):
                for way in range(2):
                    last = 4 if way == 0 else 3
                    if i <= last:
                        block = self.zwait(way, i, piece)
                        if piece == 0:
                            blocks.append(block)
                        if i < last:
                            self.zsend(way, i + 1, piece)
            for way, block in enumerate(blocks):
                self.dsend(2 * i - 1 + way, block)

        def settle(self, i):
            if i == 1:
                self.dwait(0, zc + sign)
            for way in range(2):
                last = 4 if way == 0 else 3
                if i <= last:
                    hop = -sign if way == 0 else sign
                    block = lax.rem(z - hop * i + NZ, NZ) * NC + (1 - c)
                    self.dwait(2 * i - 1 + way, block)

    table_own = Gather(0, tt.at[0])
    table_far = Gather(1, tt.at[1])
    outw = Gather(2, wt)

    send(tt.at[0, zc, x], tt.at[1, zc, x], t2_s, t2_r, at_y(2))
    table_own.first()
    bands(0, lf_ref)

    copy(tok_ref, tprev, tok_s, tok_r, mate).wait_recv()
    for tile in range(2):
        row = tprev[tile + 6 : tile + 7, :]
        row = jnp.where(s == 0, -1, row)
        oneh[:, tile * 128 : (tile + 1) * 128] = jnp.where(ids == row, 1.0, 0.0).astype(BF16)

    pair0 = z // 2
    even = 1 - 2 * lax.rem(z, 2)

    def pair(i):
        move = (0, -even, even, 2)[i - 1]
        return lax.rem(pair0 + move + 4, 4)

    lane = lax.broadcasted_iota(jnp.int32, (16, 128), 1)

    def fir(rows, tap, first):
        f = [jnp.broadcast_to(tap[:, n : n + 1], (16, 128)) for n in range(7)]
        outs = {}
        for tile in range(first - 1, TILES):
            cur = proj[pl.ds(rows, 16), tile * 128 : (tile + 1) * 128]
            turn = [pltpu.roll(cur, n, 1) for n in (1, 2, 3)]
            if tile >= first:
                lag = [jnp.where(lane < n + 1, old[n], turn[n]) for n in range(3)]
            else:
                lag = turn
            late = f[4] * cur + f[5] * lag[0] + f[6] * lag[1]
            late = pltpu.roll(late, 4, 1)
            if tile >= first:
                outs[tile] = (
                    f[0] * cur + f[1] * lag[0] + f[2] * lag[1] + f[3] * lag[2]
                    + jnp.where(lane < 4, oldlate, late)
                )
            old, oldlate = turn, late
        return outs

    def block(which, k, p):
        left = jnp.concatenate(
            [tt[which, pl.ds(4 * p, 4), b].reshape(384, 128) for b in range(NX)], axis=1
        )
        for n in range(5):
            proj[:, n * 256 : (n + 1) * 256] = jnp.dot(
                left, oneh[:, n * 256 : (n + 1) * 256], preferred_element_type=F32
            )

        def group(g, carry):
            ch = pl.multiple_of(g * 16, 16)
            base = (g // 2) * 96 + lax.rem(g, 2) * 16
            tap = [taps[which, p, part, pl.ds(ch, 16), :] for part in range(3)]
            key = fir(pl.multiple_of(base + 32, 16), tap[1], 1)
            val = fir(pl.multiple_of(base + 64, 16), tap[2], 1)
            prod = {tile: (key[tile] * val[tile]).astype(BF16) for tile in key}
            rows = jnp.concatenate(
                [jnp.concatenate([prod[t - 1], prod[t]], axis=1) for t in range(2, TILES)], axis=0
            )
            conv = jnp.dot(rows, band[which, 8 * p + g], preferred_element_type=F32)
            query = fir(pl.multiple_of(base, 16), tap[0], 2)
            skip = jnp.broadcast_to(tap[0][:, 7:8], (16, 128))
            for t in range(2, TILES):
                whole = conv[(t - 2) * 16 : (t - 1) * 16] + skip * prod[t].astype(F32)
                g4[k, p, pl.ds(ch, 16), (t - 2) * 128 : (t - 1) * 128] = (
                    query[t] * whole
                ).astype(BF16)
            return carry

        lax.fori_loop(0, 8, group, 0)

    def gsend(i):
        p = pair(i)
        here = g4.at[y, p]
        for way, q in ((0, 1), (1, 3)):
            send(here, here, g_s.at[way, i - 1], g_r.at[way, i - 1], at_y(q))

    def gwait(i):
        p = pair(i)
        for way, q in ((0, 3), (1, 1)):
            here = g4.at[lax.rem(y + q, NY), p]
            copy(here, here, g_s.at[way, i - 1], g_r.at[way, i - 1], mate).wait_recv()

    def own(i):
        table_own.settle(i)
        block(0, y, pair(i))
        gsend(i)

    def others(i):
        table_far.settle(i)
        block(1, far, pair(i))

    table_own.step(1)
    own(1)
    table_own.step(2)
    copy(tt.at[0, zc, x], tt.at[1, zc, x], t2_s, t2_r, mate).wait_recv()
    table_far.first()
    own(2)
    table_own.step(3)
    table_far.step(1)

    @pl.when(x != y)
    def _():
        copy(wo_ref, wt.at[zc, x], wo_s, wo_r, mate).wait()

    outw.first()
    own(3)
    table_own.step(4)
    table_far.step(2)
    outw.step(1)
    own(4)
    table_far.step(3)
    outw.step(2)
    for n in range(2):
        ref = (sf2, lf2)[n]
        copy(ref, ref, fil_s.at[n], fil_r.at[n], mate).wait_recv()
    columns(1, sf2)
    bands(1, lf2)
    others(1)
    table_far.step(4)
    outw.step(3)
    others(2)
    outw.step(4)
    others(3)
    others(4)
    for i in range(1, 5):
        outw.settle(i)

    def project(ks, n):
        sums = None
        for k in ks:
            left = jnp.concatenate(
                [wt[pl.ds(4 * n, 4), k, p].reshape(128, 128) for p in range(4)], axis=1
            )
            term = jnp.dot(left, g4[k].reshape(512, 1024), preferred_element_type=F32)
            sums = term if sums is None else sums + term
        return sums

    def near(n, carry):
        cols = pl.ds(pl.multiple_of(n * 128, 128), 128)
        resid = lax.dot_general(
            emb_ref[:, cols], oneh[:, 256:], (((0,), (0,)), ((), ())), preferred_element_type=F32
        )
        acc[cols, :] = resid + project((y, far), n)
        return carry

    lax.fori_loop(0, 4, near, 0)
    for i in range(1, 5):
        gwait(i)

    def rest(n, carry):
        rows = pl.ds(pl.multiple_of(n * 128, 128), 128)
        ks = (lax.rem(y + 1, NY), lax.rem(y + 3, NY))
        out_ref[rows, :] = (acc[rows, :] + project(ks, n)).astype(BF16)
        return carry

    lax.fori_loop(0, 4, rest, 0)
    for one in sent:
        one.wait_send()


def body(
    token_ids, embed_table, norm_gain, in_weight, short_filter, long_filter, long_skip, out_weight
):
    tok = token_ids.reshape(8, 128)
    gain = norm_gain.reshape(4, 1, 512)
    w = in_weight.reshape(32, 3, 16, 32).transpose(2, 0, 1, 3).reshape(16, 32, 96)
    w = jnp.pad(w, ((0, 0), (0, 0), (0, 32)))
    wo = out_weight.T.reshape(32, 4, 128).transpose(1, 0, 2)
    skip = jnp.broadcast_to(long_skip[None, None, :], (1, 3, 512))
    sf = jnp.concatenate([short_filter, skip], axis=0)
    sf = sf.reshape(8, 3, 4, 128).transpose(2, 1, 0, 3)
    lf = long_filter.astype(F32)
    vmem = pl.BlockSpec(memory_space=pltpu.VMEM)
    dma = pltpu.SemaphoreType.DMA
    out = pl.pallas_call(
        kernel,
        out_shape=jax.ShapeDtypeStruct((512, 1024), BF16),
        in_specs=[vmem] * 7,
        out_specs=vmem,
        scratch_shapes=[
            pltpu.VMEM((8, 128), jnp.int32),
            pltpu.VMEM((4, 3, 8, 128), F32),
            pltpu.VMEM((32, 128), F32),
            pltpu.VMEM((NX, LINE, 32, 128), BF16),
            pltpu.VMEM((NY, 128, 512), BF16),
            pltpu.VMEM((2, LINE, NX, 96, 128), BF16),
            pltpu.VMEM((LINE, NX, 4, 32, 128), BF16),
            pltpu.VMEM((NY, 4, 128, 1024), BF16),
            pltpu.VMEM((512, TILES * 128), BF16),
            pltpu.VMEM((2, 32, 256, 128), BF16),
            pltpu.VMEM((2, 4, 3, 128, 8), F32),
            pltpu.VMEM((384, TILES * 128), F32),
            pltpu.VMEM((512, 1024), F32),
            dma, dma, dma((2,)), dma((2,)), dma((LINE - 1,)), dma((LINE - 1,)),
            dma((3,)), dma((3,)), dma((3,)), dma((3,)), dma, dma, dma, dma,
            dma((3, 3)), dma((3, 3)), dma((3, 2, 4, 4)), dma((3, 2, 4, 4)),
            dma((3, 8)), dma((3, 8)), dma((2, 4)), dma((2, 4)),
        ],
        compiler_params=pltpu.CompilerParams(
            collective_id=0, has_side_effects=True, vmem_limit_bytes=60 * 2**20
        ),
    )(tok, embed_table, gain, w, wo, sf, lf)
    return out.T


def solution(mesh):
    placed = (
        P("seq"),
        P(None, "tp"),
        P(),
        P("seq", None, "tp"),
        P(None, None, "tp"),
        P("tp", None),
        P("tp"),
        P("tp", "seq"),
    )
    return jax.shard_map(
        body, mesh=mesh, in_specs=placed, out_specs=P("seq", "tp"), check_vma=False
    )
```

```python
import functools

import jax
import jax.numpy as jnp
from jax import lax
from jax.experimental import pallas as pl
from jax.experimental.pallas import tpu as pltpu
from jax.sharding import PartitionSpec as P

MESH = pl.DeviceIdType.MESH
BF16 = jnp.bfloat16
F32 = jnp.float32
NX, NZ, NC, NY = 4, 8, 2, 4
LINE = NZ * NC
TILES = 10


def kernel(
    tok_ref, emb_ref, gain_ref, w_ref, wo_ref, short_ref, skip_ref, long_ref, out_ref,
    tprev, sf, lf, wsend, wosend, wl, e4, tt, wt, g4, oneh, band, taps, proj, acc, stage,
    tok_s, tok_r, fil_s, fil_r, s1_s, s1_r, s2_s, s2_r, e_s, e_r, wo_s, wo_r, t2_s, t2_r,
    ax_s, ax_r, az_s, az_r, ad_s, ad_r, g_s, g_r, out_s,
):
    s = lax.axis_index("seq")
    y = lax.axis_index("tp")
    zc = lax.rem(s, LINE)
    x = s // LINE
    z = zc // NC
    c = lax.rem(zc, NC)
    sign = 1 - 2 * c
    far = lax.rem(y + 2, NY)
    turned = y * LINE + zc

    def at_x(q):
        return (lax.rem(x + q, NX) * LINE + zc, y)

    def at_y(q):
        return (s, lax.rem(y + q, NY))

    def at_z(q):
        return (x * LINE + lax.rem(z + q + NZ, NZ) * NC + c, y)

    mate = (s + sign, y)
    after = (lax.rem(s + 1, NX * LINE), y)
    before = (lax.rem(s + NX * LINE - 1, NX * LINE), y)

    sent = []

    def copy(src, dst, ss, rs, dev):
        return pltpu.make_async_remote_copy(
            src_ref=src, dst_ref=dst, send_sem=ss, recv_sem=rs, device_id=dev, device_id_type=MESH
        )

    def send(*args):
        one = copy(*args)
        one.start()
        sent.append(one)

    hello = pltpu.get_barrier_semaphore()
    greeted = 0
    for r in range(1, LINE):
        pl.semaphore_signal(
            hello, inc=1, device_id=(x * LINE + lax.rem(zc + r, LINE), y), device_id_type=MESH
        )
        greeted += 1
    for r in range(1, NX):
        pl.semaphore_signal(hello, inc=1, device_id=at_x(r), device_id_type=MESH)
        pl.semaphore_signal(hello, inc=1, device_id=at_y(r), device_id_type=MESH)
        greeted += 2
    pl.semaphore_signal(hello, inc=1, device_id=after, device_id_type=MESH)
    pl.semaphore_signal(hello, inc=1, device_id=before, device_id_type=MESH)
    greeted += 2

    @pl.when(x != y)
    def _():
        pl.semaphore_signal(hello, inc=1, device_id=(turned, x), device_id_type=MESH)

    lane32 = lax.broadcasted_iota(jnp.int32, (32, 128), 1) // 32
    for p in range(4):
        chunk = [w_ref[part, :, p * 128 : (p + 1) * 128] for part in range(3)]
        for n in range(4):
            moved = [
                chunk[part] if part == n else pltpu.roll(chunk[part], (part - n) % 4 * 32, 1)
                for part in range(3)
            ]
            wsend[4 * p + n] = jnp.where(
                lane32 == 0, moved[0], jnp.where(lane32 == 1, moved[1], moved[2])
            )
        wosend[p] = wo_ref[:, p * 128 : (p + 1) * 128]
        for part in range(3):
            sf[0, p, part, 0:7, :] = short_ref[part, :, p * 128 : (p + 1) * 128]
            sf[0, p, part, 7:8, :] = skip_ref[:, p * 128 : (p + 1) * 128]
    lf[0] = long_ref[...].astype(F32)
    wl[x, zc] = wsend[zc]
    e4[y] = emb_ref[pl.ds(pl.multiple_of(x * 128, 128), 128), :]

    @pl.when(x == y)
    def _():
        wt[zc, x] = wosend[...]

    ids = lax.broadcasted_iota(jnp.int32, (512, 128), 0)
    for tile in range(8):
        row = tok_ref[tile : tile + 1, :]
        oneh[:, (tile + 2) * 128 : (tile + 3) * 128] = (
            jnp.where(ids == row, 1.0, 0.0).astype(BF16)
        )

    above = lax.broadcasted_iota(jnp.int32, (128, 128), 1) >= lax.broadcasted_iota(
        jnp.int32, (128, 128), 0
    )

    def bands(which):
        def build(g, carry):
            rows = jnp.broadcast_to(lf[which, pl.ds(g, 1), :], (128, 128))
            moved = pltpu.roll(rows, 0, 1, stride=1, stride_axis=0)
            band[which, g, 0:128, :] = jnp.where(above, 0.0, moved).astype(BF16)
            band[which, g, 128:256, :] = jnp.where(above, moved, 0.0).astype(BF16)
            return carry

        lax.fori_loop(0, 32, build, 0)

    def columns(which):
        for p in range(4):
            for part in range(3):
                taps[which, p, part] = sf[which, p, part].T

    columns(0)
    bands(0)
    pl.semaphore_wait(hello, greeted + jnp.where(x == y, 0, 1))

    half = pl.ds(pl.multiple_of(64 * c, 64), 64)
    other = pl.ds(pl.multiple_of(64 - 64 * c, 64), 64)
    for r in (8, 7, 9, 6, 10, 5, 11, 4, 12, 3, 13, 2, 14, 1, 15):
        to = lax.rem(zc + r, LINE)
        send(wsend.at[to], wl.at[x, zc], s1_s.at[r - 1], s1_r.at[r - 1], (x * LINE + to, y))
    for r in (2, 1, 3):
        send(
            emb_ref.at[pl.ds(pl.multiple_of(x * 128 + 64 * c, 64), 64)],
            e4.at[y, half], e_s.at[0, r - 1], e_r.at[0, r - 1], at_y(r),
        )
    send(tok_ref, tprev, tok_s, tok_r, after)
    send(sf.at[0], sf.at[1], fil_s.at[0], fil_r.at[0], at_y(2))
    send(lf.at[0], lf.at[1], fil_s.at[1], fil_r.at[1], at_y(2))

    @pl.when(x != y)
    def _():
        copy(wosend, wt.at[zc, y], wo_s, wo_r, (turned, x)).start()

    for r in range(1, LINE):
        here = wl.at[x, lax.rem(zc + LINE - r, LINE)]
        copy(here, here, s1_s.at[r - 1], s1_r.at[r - 1], mate).wait_recv()

    parts = (pl.ds(0, 8), pl.ds(8, 8))
    for way, q in ((0, 1), (1, 3)):
        for n in (way, 1 - way):
            here = wl.at[x, parts[n]]
            send(here, here, s2_s.at[way, n], s2_r.at[way, n], at_x(q))
    for r in (1, 3, 2):
        here = e4.at[lax.rem(y + NY - r, NY), half]
        copy(here, here, e_s.at[0, r - 1], e_r.at[0, r - 1], mate).wait_recv()
        send(here, here, e_s.at[1, r - 1], e_r.at[1, r - 1], mate)
    for way, q in ((0, 1), (1, 3)):
        here = wl.at[lax.rem(x + NX - q, NX), parts[way]]
        copy(here, here, s2_s.at[way, way], s2_r.at[way, way], mate).wait_recv()
        send(here, here, s2_s.at[2, way], s2_r.at[2, way], at_x(q))
    for n in range(2):
        ref = (sf, lf)[n].at[1]
        copy(ref, ref, fil_s.at[n], fil_r.at[n], mate).wait_recv()
    columns(1)
    bands(1)
    for r in (1, 3, 2):
        here = e4.at[lax.rem(y + NY - r, NY), other]
        copy(here, here, e_s.at[1, r - 1], e_r.at[1, r - 1], mate).wait_recv()

    total = jnp.zeros((128, 1), F32)
    for k in range(NY):
        piece = e4[k].astype(F32)
        total = total + jnp.sum(piece * piece, axis=1, keepdims=True)
    scale = lax.rsqrt(total * (1.0 / 2048) + 1e-06)
    normed = [
        (e4[k].astype(F32) * scale * gain_ref[k]).astype(BF16) for k in range(NY)
    ]
    copy(tok_ref, tprev, tok_s, tok_r, mate).wait_recv()
    for tile in range(2):
        row = tprev[tile + 6 : tile + 7, :]
        row = jnp.where(s == 0, -1, row)
        oneh[:, tile * 128 : (tile + 1) * 128] = jnp.where(ids == row, 1.0, 0.0).astype(BF16)

    for way, q in ((0, 1), (1, 3)):
        here = wl.at[lax.rem(x + NX - q, NX), parts[1 - way]]
        copy(here, here, s2_s.at[way, 1 - way], s2_r.at[way, 1 - way], mate).wait_recv()
    for way in range(2):
        here = wl.at[lax.rem(x + 2, NX), parts[way]]
        copy(here, here, s2_s.at[2, way], s2_r.at[2, way], mate).wait_recv()
    table = jnp.zeros((128, 128), F32)
    for k in range(NX):
        table = table + jnp.dot(
            normed[k], wl[k].reshape(512, 128), preferred_element_type=F32
        )
    tt[0, zc, x] = table.T[0:96].astype(BF16)

    class Gather:
        def __init__(self, n, buf):
            self.n, self.buf = n, buf

        def xsend(self):
            for q in range(1, NX):
                here = self.buf.at[zc, x]
                send(here, here, ax_s.at[self.n, q - 1], ax_r.at[self.n, q - 1], at_x(q))

        def zsend(self, way, step, piece):
            hop = sign if way == 0 else -sign
            block = lax.rem(z - hop * (step - 1) + NZ, NZ) * NC + c
            here = self.buf.at[block, lax.rem(x + NX - piece, NX)]
            at = (self.n, way, step - 1, piece)
            send(here, here, az_s.at[at], az_r.at[at], at_z(hop))

        def zwait(self, way, step, piece):
            hop = sign if way == 0 else -sign
            block = lax.rem(z - hop * step + NZ, NZ) * NC + c
            here = self.buf.at[block, lax.rem(x + NX - piece, NX)]
            at = (self.n, way, step - 1, piece)
            copy(here, here, az_s.at[at], az_r.at[at], mate).wait_recv()
            return block

        def dsend(self, slot, block):
            here = self.buf.at[block]
            send(here, here, ad_s.at[self.n, slot], ad_r.at[self.n, slot], mate)

        def dwait(self, slot, block):
            here = self.buf.at[block]
            copy(here, here, ad_s.at[self.n, slot], ad_r.at[self.n, slot], mate).wait_recv()

        def first(self):
            for piece in range(NX):
                if piece:
                    there = self.buf.at[zc, lax.rem(x + NX - piece, NX)]
                    copy(there, there, ax_s.at[self.n, piece - 1], ax_r.at[self.n, piece - 1], mate).wait_recv()
                self.zsend(0, 1, piece)
                self.zsend(1, 1, piece)
            self.dsend(0, zc)

        def step(self, i):
            blocks = []
            for piece in range(NX):
                for way in range(2):
                    last = 4 if way == 0 else 3
                    if i <= last:
                        block = self.zwait(way, i, piece)
                        if piece == 0:
                            blocks.append(block)
                        if i < last:
                            self.zsend(way, i + 1, piece)
            for way, block in enumerate(blocks):
                self.dsend(2 * i - 1 + way, block)

        def settle(self, i):
            if i == 1:
                self.dwait(0, zc + sign)
            for way in range(2):
                last = 4 if way == 0 else 3
                if i <= last:
                    hop = -sign if way == 0 else sign
                    block = lax.rem(z - hop * i + NZ, NZ) * NC + (1 - c)
                    self.dwait(2 * i - 1 + way, block)

    table_own = Gather(0, tt.at[0])
    table_far = Gather(1, tt.at[1])
    outw = Gather(2, wt)

    send(tt.at[0, zc, x], tt.at[1, zc, x], t2_s, t2_r, at_y(2))
    table_own.xsend()
    table_own.first()

    @pl.when(x != y)
    def _():
        copy(wosend, wt.at[zc, x], wo_s, wo_r, mate).wait()

    outw.xsend()

    pair0 = z // 2
    even = 1 - 2 * lax.rem(z, 2)

    def pair(i):
        move = (0, -even, even, 2)[i - 1]
        return lax.rem(pair0 + move + 4, 4)

    lane = lax.broadcasted_iota(jnp.int32, (16, 128), 1)

    def fir(rows, tap, first):
        f = [jnp.broadcast_to(tap[:, n : n + 1], (16, 128)).astype(BF16) for n in range(7)]
        outs = {}
        for tile in range(first - 1, TILES):
            cur = proj[pl.ds(rows, 16), tile * 128 : (tile + 1) * 128]
            turn = [pltpu.roll(cur, n, 1) for n in (1, 2, 3)]
            if tile >= first:
                lag = [jnp.where(lane < n + 1, old[n], turn[n]) for n in range(3)]
            else:
                lag = turn
            late = f[4] * cur + f[5] * lag[0] + f[6] * lag[1]
            late = pltpu.roll(late, 4, 1)
            if tile >= first:
                outs[tile] = (
                    f[0] * cur + f[1] * lag[0] + f[2] * lag[1] + f[3] * lag[2]
                    + jnp.where(lane < 4, oldlate, late)
                )
            old, oldlate = turn, late
        return outs

    def block(which, k, p):
        left = jnp.concatenate(
            [tt[which, pl.ds(4 * p, 4), b].reshape(384, 128) for b in range(NX)], axis=1
        )
        for n in range(5):
            proj[:, n * 256 : (n + 1) * 256] = jnp.dot(
                left, oneh[:, n * 256 : (n + 1) * 256], preferred_element_type=F32
            ).astype(BF16)

        def group(g, carry):
            ch = pl.multiple_of(g * 16, 16)
            base = (g // 2) * 96 + lax.rem(g, 2) * 16
            tap = [taps[which, p, part, pl.ds(ch, 16), :] for part in range(3)]
            key = fir(pl.multiple_of(base + 32, 16), tap[1], 1)
            val = fir(pl.multiple_of(base + 64, 16), tap[2], 1)
            prod = {tile: key[tile] * val[tile] for tile in key}
            rows = jnp.concatenate(
                [jnp.concatenate([prod[t - 1], prod[t]], axis=1) for t in range(2, TILES)], axis=0
            )
            conv = jnp.dot(rows, band[which, 8 * p + g], preferred_element_type=F32).astype(BF16)
            query = fir(pl.multiple_of(base, 16), tap[0], 2)
            skip = jnp.broadcast_to(tap[0][:, 7:8], (16, 128)).astype(BF16)
            for t in range(2, TILES):
                whole = conv[(t - 2) * 16 : (t - 1) * 16] + skip * prod[t]
                g4[k, p, pl.ds(ch, 16), (t - 2) * 128 : (t - 1) * 128] = query[t] * whole
            return carry

        lax.fori_loop(0, 8, group, 0)

    def gsend(i):
        p = pair(i)
        here = g4.at[y, p]
        for way, q in ((0, 1), (1, 3)):
            send(here, here, g_s.at[way, i - 1], g_r.at[way, i - 1], at_y(q))

    def gwait(i):
        p = pair(i)
        for way, q in ((0, 3), (1, 1)):
            here = g4.at[lax.rem(y + q, NY), p]
            copy(here, here, g_s.at[way, i - 1], g_r.at[way, i - 1], mate).wait_recv()

    def own(i):
        table_own.settle(i)
        block(0, y, pair(i))
        gsend(i)

    def others(i):
        table_far.settle(i)
        block(1, far, pair(i))

    table_own.step(1)
    copy(tt.at[0, zc, x], tt.at[1, zc, x], t2_s, t2_r, mate).wait_recv()
    table_far.xsend()
    own(1)
    table_own.step(2)
    table_far.first()
    own(2)
    table_own.step(3)
    table_far.step(1)
    own(3)
    table_own.step(4)
    table_far.step(2)
    outw.first()
    own(4)
    table_far.step(3)
    outw.step(1)
    others(1)
    table_far.step(4)
    outw.step(2)
    others(2)
    outw.step(3)
    others(3)
    outw.step(4)
    others(4)
    for i in range(1, 5):
        outw.settle(i)

    def project(ks, n):
        sums = None
        for k in ks:
            left = jnp.concatenate(
                [wt[pl.ds(4 * n, 4), k, p].reshape(128, 128) for p in range(4)], axis=1
            )
            term = jnp.dot(left, g4[k].reshape(512, 1024), preferred_element_type=F32)
            sums = term if sums is None else sums + term
        return sums

    def near(n, carry):
        cols = pl.ds(pl.multiple_of(n * 128, 128), 128)
        resid = lax.dot_general(
            emb_ref[:, cols], oneh[:, 256:], (((0,), (0,)), ((), ())), preferred_element_type=F32
        )
        acc[cols, :] = resid + project((y, far), n)
        return carry

    lax.fori_loop(0, 4, near, 0)
    for i in range(1, 5):
        gwait(i)

    def written(n):
        rows = pl.ds(pl.multiple_of(n * 128, 128), 128)
        return pltpu.make_async_copy(stage.at[rows], out_ref.at[rows], out_s.at[n])

    def rest(n, carry):
        rows = pl.ds(pl.multiple_of(n * 128, 128), 128)
        ks = (lax.rem(y + 1, NY), lax.rem(y + 3, NY))
        stage[rows, :] = (acc[rows, :] + project(ks, n)).astype(BF16)
        written(n).start()
        return carry

    lax.fori_loop(0, 4, rest, 0)
    for one in sent:
        one.wait_send()
    for n in range(4):
        written(n).wait()


def body(
    token_ids, embed_table, norm_gain, in_weight, short_filter, long_filter, long_skip, out_weight
):
    tok = token_ids.reshape(8, 128)
    gain = norm_gain.reshape(4, 1, 512)
    w = in_weight.transpose(1, 0, 2)
    short = short_filter.transpose(1, 0, 2)
    skip = long_skip.reshape(1, 512)
    vmem = pl.BlockSpec(memory_space=pltpu.VMEM)
    dma = pltpu.SemaphoreType.DMA
    out = pl.pallas_call(
        kernel,
        out_shape=jax.ShapeDtypeStruct((512, 1024), BF16),
        in_specs=[vmem] * 8,
        out_specs=pl.BlockSpec(memory_space=pl.ANY),
        scratch_shapes=[
            pltpu.VMEM((8, 128), jnp.int32),
            pltpu.VMEM((2, 4, 3, 8, 128), F32),
            pltpu.VMEM((2, 32, 128), F32),
            pltpu.VMEM((LINE, 32, 128), BF16),
            pltpu.VMEM((4, 32, 128), BF16),
            pltpu.VMEM((NX, LINE, 32, 128), BF16),
            pltpu.VMEM((NY, 128, 512), BF16),
            pltpu.VMEM((2, LINE, NX, 96, 128), BF16),
            pltpu.VMEM((LINE, NX, 4, 32, 128), BF16),
            pltpu.VMEM((NY, 4, 128, 1024), BF16),
            pltpu.VMEM((512, TILES * 128), BF16),
            pltpu.VMEM((2, 32, 256, 128), BF16),
            pltpu.VMEM((2, 4, 3, 128, 8), F32),
            pltpu.VMEM((384, TILES * 128), BF16),
            pltpu.VMEM((512, 1024), F32),
            pltpu.VMEM((512, 1024), BF16),
            dma, dma, dma((2,)), dma((2,)), dma((LINE - 1,)), dma((LINE - 1,)),
            dma((3, 2)), dma((3, 2)), dma((2, 3)), dma((2, 3)), dma, dma, dma, dma,
            dma((3, 3)), dma((3, 3)), dma((3, 2, 4, 4)), dma((3, 2, 4, 4)),
            dma((3, 8)), dma((3, 8)), dma((2, 4)), dma((2, 4)), dma((4,)),
        ],
        compiler_params=pltpu.CompilerParams(
            collective_id=0, has_side_effects=True, vmem_limit_bytes=60 * 2**20
        ),
    )(tok, embed_table, gain, w, out_weight.T, short, skip, long_filter)
    return out.T


def solution(mesh):
    placed = (
        P("seq"),
        P(None, "tp"),
        P(),
        P("seq", None, "tp"),
        P(None, None, "tp"),
        P("tp", None),
        P("tp"),
        P("tp", "seq"),
    )
    return jax.shard_map(
        body, mesh=mesh, in_specs=placed, out_specs=P("seq", "tp"), check_vma=False
    )
```

```python
import functools

import jax
import jax.numpy as jnp
from jax import lax
from jax.experimental import pallas as pl
from jax.experimental.pallas import tpu as pltpu
from jax.sharding import PartitionSpec as P

MESH = pl.DeviceIdType.MESH
BF16 = jnp.bfloat16
F32 = jnp.float32
NX, NZ, NC, NY = 4, 8, 2, 4
LINE = NZ * NC
TILES = 10


def kernel(
    tok_ref, emb_ref, gain_ref, w_ref, wo_ref, short_ref, skip_ref, long_ref, out_ref,
    tprev, sf, lf, wsend, wosend, wl, e4, tt, wt, g4, oneh, band, taps, tabn, proj, pt, qt, acc, stage,
    tok_s, tok_r, fil_s, fil_r, s1_s, s1_r, s2_s, s2_r, e_s, e_r, wo_s, wo_r, t2_s, t2_r,
    ax_s, ax_r, az_s, az_r, ad_s, ad_r, g_s, g_r, out_s,
):
    s = lax.axis_index("seq")
    y = lax.axis_index("tp")
    zc = lax.rem(s, LINE)
    x = s // LINE
    z = zc // NC
    c = lax.rem(zc, NC)
    sign = 1 - 2 * c
    far = lax.rem(y + 2, NY)
    turned = y * LINE + zc

    def at_x(q):
        return (lax.rem(x + q, NX) * LINE + zc, y)

    def at_y(q):
        return (s, lax.rem(y + q, NY))

    def at_z(q):
        return (x * LINE + lax.rem(z + q + NZ, NZ) * NC + c, y)

    mate = (s + sign, y)
    after = (lax.rem(s + 1, NX * LINE), y)
    before = (lax.rem(s + NX * LINE - 1, NX * LINE), y)

    def copy(src, dst, ss, rs, dev):
        return pltpu.make_async_remote_copy(
            src_ref=src, dst_ref=dst, send_sem=ss, recv_sem=rs, device_id=dev, device_id_type=MESH
        )

    def send(*args):
        copy(*args).start()

    def got(ref, rs):
        copy(ref, ref, tok_s, rs, mate).wait_recv()

    def gone(ref, ss):
        copy(ref, ref, ss, tok_r, mate).wait_send()

    hello = pltpu.get_barrier_semaphore()
    greeted = 0
    for r in range(1, LINE):
        pl.semaphore_signal(
            hello, inc=1, device_id=(x * LINE + lax.rem(zc + r, LINE), y), device_id_type=MESH
        )
        greeted += 1
    for r in range(1, NX):
        pl.semaphore_signal(hello, inc=1, device_id=at_x(r), device_id_type=MESH)
        pl.semaphore_signal(hello, inc=1, device_id=at_y(r), device_id_type=MESH)
        greeted += 2
    pl.semaphore_signal(hello, inc=1, device_id=after, device_id_type=MESH)
    pl.semaphore_signal(hello, inc=1, device_id=before, device_id_type=MESH)
    greeted += 2

    @pl.when(x != y)
    def _():
        pl.semaphore_signal(hello, inc=1, device_id=(turned, x), device_id_type=MESH)

    lane32 = lax.broadcasted_iota(jnp.int32, (32, 128), 1) // 32
    for p in range(4):
        chunk = [w_ref[part, :, p * 128 : (p + 1) * 128] for part in range(3)]
        for n in range(4):
            moved = [
                chunk[part] if part == n else pltpu.roll(chunk[part], (part - n) % 4 * 32, 1)
                for part in range(3)
            ]
            wsend[4 * p + n] = jnp.where(
                lane32 == 0, moved[0], jnp.where(lane32 == 1, moved[1], moved[2])
            )
        wosend[p] = wo_ref[:, p * 128 : (p + 1) * 128]
        for part in range(3):
            sf[0, p, part, 0:7, :] = short_ref[part, :, p * 128 : (p + 1) * 128]
            sf[0, p, part, 7:8, :] = skip_ref[:, p * 128 : (p + 1) * 128]
    lf[0] = long_ref[...].astype(F32)
    wl[x, zc] = wsend[zc]
    e4[y] = emb_ref[pl.ds(pl.multiple_of(x * 128, 128), 128), :]

    @pl.when(x == y)
    def _():
        wt[zc, x] = wosend[...]

    ids = lax.broadcasted_iota(jnp.int32, (128, 512), 1)

    def onehot(tile, column):
        oneh[tile * 128 : (tile + 1) * 128, :] = jnp.where(
            ids == jnp.broadcast_to(column, (128, 512)), 1.0, 0.0
        ).astype(BF16)

    names = tok_ref[...].T
    for tile in range(8):
        onehot(tile + 2, names[:, tile : tile + 1])

    above = lax.broadcasted_iota(jnp.int32, (128, 128), 1) >= lax.broadcasted_iota(
        jnp.int32, (128, 128), 0
    )

    def bands(which, begin, end):
        def build(g, carry):
            rows = jnp.broadcast_to(lf[which, pl.ds(g, 1), :], (128, 128))
            moved = pltpu.roll(rows, 0, 1, stride=1, stride_axis=0)
            band[which, g, 0:128, :] = jnp.where(above, 0.0, moved).astype(BF16)
            band[which, g, 128:256, :] = jnp.where(above, moved, 0.0).astype(BF16)
            return carry

        lax.fori_loop(begin, end, build, 0)

    def columns(which):
        for p in range(4):
            taps[which, p] = sf[which, p, 0].T

    columns(0)
    bands(0, 0, 32)
    pl.semaphore_wait(hello, greeted + jnp.where(x == y, 0, 1))

    half = pl.ds(pl.multiple_of(64 * c, 64), 64)
    other = pl.ds(pl.multiple_of(64 - 64 * c, 64), 64)
    for r in (8, 7, 9, 6, 10, 5, 11, 4, 12, 3, 13, 2, 14, 1, 15):
        to = lax.rem(zc + r, LINE)
        send(wsend.at[to], wl.at[x, zc], s1_s, s1_r, (x * LINE + to, y))
    for r in (2, 1, 3):
        send(
            emb_ref.at[pl.ds(pl.multiple_of(x * 128 + 64 * c, 64), 64)],
            e4.at[y, half], e_s.at[0], e_r.at[r - 1], at_y(r),
        )
    send(tok_ref, tprev, tok_s, tok_r, after)
    send(sf.at[0], sf.at[1], fil_s.at[0], fil_r.at[0], at_y(2))
    send(lf.at[0], lf.at[1], fil_s.at[1], fil_r.at[1], at_y(2))

    @pl.when(x != y)
    def _():
        copy(wosend, wt.at[zc, y], wo_s, wo_r, (turned, x)).start()

    got(wl.at[x, pl.ds(0, LINE - 1)], s1_r)

    parts = (pl.ds(0, 8), pl.ds(8, 8))
    for way, q in ((0, 1), (1, 3)):
        for n in (way, 1 - way):
            here = wl.at[x, parts[n]]
            send(here, here, s2_s, s2_r.at[way, n], at_x(q))
    for r in (1, 3, 2):
        here = e4.at[lax.rem(y + NY - r, NY), half]
        got(here, e_r.at[r - 1])
        send(here, here, e_s.at[1], e_r.at[3], mate)
    for way, q in ((0, 1), (1, 3)):
        here = wl.at[lax.rem(x + NX - q, NX), parts[way]]
        got(here, s2_r.at[way, way])
        send(here, here, s2_s, s2_r.at[2, way], at_x(q))
    got(e4.at[pl.ds(0, 3), other], e_r.at[3])

    total = jnp.zeros((128, 1), F32)
    for k in range(NY):
        piece = e4[k].astype(F32)
        total = total + jnp.sum(piece * piece, axis=1, keepdims=True)
    scale = lax.rsqrt(total * (1.0 / 2048) + 1e-06)
    normed = [
        (e4[k].astype(F32) * scale * gain_ref[k]).astype(BF16) for k in range(NY)
    ]
    got(tprev, tok_r)
    names = jnp.where(s == 0, -1, tprev[...]).T
    for tile in range(2):
        onehot(tile, names[:, tile + 6 : tile + 7])

    for way, q in ((0, 1), (1, 3)):
        here = wl.at[lax.rem(x + NX - q, NX), parts[1 - way]]
        got(here, s2_r.at[way, 1 - way])
    for way in range(2):
        here = wl.at[lax.rem(x + 2, NX), parts[way]]
        got(here, s2_r.at[2, way])
    table = jnp.zeros((128, 128), F32)
    for k in range(NX):
        table = table + jnp.dot(
            normed[k], wl[k].reshape(512, 128), preferred_element_type=F32
        )
    tt[0, zc, x] = table.T[0:96].astype(BF16)

    class Gather:
        def __init__(self, n, buf):
            self.n, self.buf = n, buf
            self.fine = n == 0
            self.units = range(NX) if self.fine else (None,)

        def ref(self, block, unit):
            if unit is None:
                return self.buf.at[block]
            return self.buf.at[block, lax.rem(x + NX - unit, NX)]

        def arrived(self, way, step, unit):
            if self.fine:
                return az_r.at[(way * 4 + step - 1) * 4 + unit]
            return az_r.at[24 + self.n * 8 + way * 4 + step - 1]

        def xsend(self):
            here = self.buf.at[zc, x]
            for q in range(1, NX):
                send(here, here, ax_s.at[self.n], ax_r.at[q - 1 if self.fine else 2 + self.n], at_x(q))

        def zsend(self, way, step, unit):
            hop = sign if way == 0 else -sign
            here = self.ref(lax.rem(z - hop * (step - 1) + NZ, NZ) * NC + c, unit)
            send(here, here, az_s.at[self.n], self.arrived(way, step, unit), at_z(hop))

        def zwait(self, way, step, unit):
            hop = sign if way == 0 else -sign
            block = lax.rem(z - hop * step + NZ, NZ) * NC + c
            got(self.ref(block, unit), self.arrived(way, step, unit))
            return block

        def dsend(self, step, block):
            here = self.buf.at[block]
            send(here, here, ad_s.at[self.n], ad_r.at[self.n, step - 1], mate)

        def first(self):
            if not self.fine:
                got(self.buf.at[zc, pl.ds(0, 3)], ax_r.at[2 + self.n])
            for unit in self.units:
                if unit:
                    got(self.ref(zc, unit), ax_r.at[unit - 1])
                self.zsend(0, 1, unit)
                self.zsend(1, 1, unit)
            self.dsend(1, zc)

        def step(self, i):
            blocks = []
            for unit in self.units:
                for way in range(2):
                    last = 4 if way == 0 else 3
                    if i <= last:
                        block = self.zwait(way, i, unit)
                        if not unit:
                            blocks.append(block)
                        if i < last:
                            self.zsend(way, i + 1, unit)
            for block in blocks:
                self.dsend(i, block)

        def settle(self, i):
            got(self.buf.at[pl.ds(0, (3, 2, 2, 1)[i - 1])], ad_r.at[self.n, i - 1])

        def close(self):
            gone(self.buf.at[0, pl.ds(0, 3)], ax_s.at[self.n])
            gone(self.buf.at[pl.ds(0, 7)], az_s.at[self.n])
            gone(self.buf.at[pl.ds(0, 8)], ad_s.at[self.n])

    table_own = Gather(0, tt.at[0])
    table_far = Gather(1, tt.at[1])
    outw = Gather(2, wt)

    table_own.xsend()
    send(tt.at[0, zc, x], tt.at[1, zc, x], t2_s, t2_r, at_y(2))
    got(sf.at[1], fil_r.at[0])
    got(lf.at[1], fil_r.at[1])
    columns(1)
    bands(1, 0, 16)
    table_own.first()

    @pl.when(x != y)
    def _():
        copy(wosend, wt.at[zc, x], wo_s, wo_r, mate).wait()

    outw.xsend()
    bands(1, 16, 32)

    pair0 = z // 2
    even = 1 - 2 * lax.rem(z, 2)

    def pair(i):
        move = (0, -even, even, 2)[i - 1]
        return lax.rem(pair0 + move + 4, 4)

    def block(which, k, p):
        table = jnp.concatenate(
            [
                jnp.concatenate(
                    [
                        tt[which, 4 * p + n, b, part * 32 : (part + 1) * 32, :]
                        for part in range(3)
                        for n in range(4)
                    ],
                    axis=0,
                )
                for b in range(NX)
            ],
            axis=1,
        )
        tabn[...] = table.T
        for n in range(5):
            rows = slice(n * 256, (n + 1) * 256)
            both = jnp.dot(oneh[rows, :], tabn[...], preferred_element_type=F32)
            for part in range(3):
                proj[part, rows, :] = both[:, part * 128 : (part + 1) * 128]

        def fir(part, row, count):
            total = None
            for lag in range(7):
                tap = jnp.broadcast_to(sf[which, p, part, lag : lag + 1, :], (count, 128))
                term = tap * proj[part, pl.ds(row - lag, count), :]
                total = term if total is None else total + term
            return total

        def tile(n, carry):
            row = pl.multiple_of(n * 128, 128)
            prod, query = [], []
            for h in range(4):
                prod.append((fir(1, row + 32 * h, 32) * fir(2, row + 32 * h, 32)).astype(BF16))
                query.append(fir(0, row + 32 * h, 32).astype(BF16))
            pt[n] = jnp.concatenate(prod, axis=0).T
            qt[n] = jnp.concatenate(query, axis=0).T
            return carry

        lax.fori_loop(1, TILES, tile, 0)

        def groups(h, carry):
            for n in range(4):
                g = 4 * h + n
                ch = pl.ds(pl.multiple_of(g * 16, 16), 16)
                prod = [pt[t, ch, :] for t in range(1, TILES)]
                rows = jnp.concatenate(
                    [jnp.concatenate([prod[t], prod[t + 1]], axis=1) for t in range(8)], axis=0
                )
                conv = jnp.dot(rows, band[which, 8 * p + g], preferred_element_type=F32).astype(BF16)
                skip = jnp.broadcast_to(taps[which, p, ch, 7:8], (16, 128)).astype(BF16)
                for t in range(8):
                    whole = conv[t * 16 : (t + 1) * 16] + skip * prod[t + 1]
                    g4[k, p, ch, t * 128 : (t + 1) * 128] = qt[t + 2, ch, :] * whole
            return carry

        lax.fori_loop(0, 2, groups, 0)

    def gsend(i):
        here = g4.at[y, pair(i)]
        for way, q in ((0, 1), (1, 3)):
            send(here, here, g_s, g_r.at[way], at_y(q))

    def own(i):
        table_own.settle(i)
        block(0, y, pair(i))
        gsend(i)

    def others(i):
        table_far.settle(i)
        block(1, far, pair(i))

    table_own.step(1)
    got(tt.at[1, zc, x], t2_r)
    table_far.xsend()
    own(1)
    table_own.step(2)
    table_far.first()
    own(2)
    table_own.step(3)
    table_far.step(1)
    own(3)
    table_own.step(4)
    table_far.step(2)
    outw.first()
    own(4)
    table_far.step(3)
    outw.step(1)
    others(1)
    table_far.step(4)
    outw.step(2)
    others(2)
    outw.step(3)
    others(3)
    outw.step(4)
    others(4)
    for i in range(1, 5):
        outw.settle(i)

    def project(ks, n):
        sums = None
        for k in ks:
            left = jnp.concatenate(
                [wt[pl.ds(4 * n, 4), k, p].reshape(128, 128) for p in range(4)], axis=1
            )
            term = jnp.dot(left, g4[k].reshape(512, 1024), preferred_element_type=F32)
            sums = term if sums is None else sums + term
        return sums

    def near(n, carry):
        cols = pl.ds(pl.multiple_of(n * 128, 128), 128)
        resid = lax.dot_general(
            emb_ref[:, cols], oneh[256:, :], (((0,), (1,)), ((), ())), preferred_element_type=F32
        )
        acc[cols, :] = resid + project((y, far), n)
        return carry

    lax.fori_loop(0, 4, near, 0)
    for way, q in ((0, 3), (1, 1)):
        got(g4.at[lax.rem(y + q, NY)], g_r.at[way])

    def rest(n, carry):
        rows = pl.ds(pl.multiple_of(n * 128, 128), 128)
        ks = (lax.rem(y + 1, NY), lax.rem(y + 3, NY))
        stage[rows, :] = (acc[rows, :] + project(ks, n)).astype(BF16)
        pltpu.make_async_copy(stage.at[rows], out_ref.at[rows], out_s).start()
        return carry

    lax.fori_loop(0, 4, rest, 0)
    gone(wsend.at[pl.ds(0, LINE - 1)], s1_s)
    gone(wl.at[pl.ds(0, 3)], s2_s)
    for n in range(2):
        gone(e4.at[pl.ds(0, 3), half], e_s.at[n])
        gone((sf, lf)[n].at[0], fil_s.at[n])
    gone(tok_ref, tok_s)
    gone(tt.at[0, zc, x], t2_s)
    gone(g4.at[pl.ds(0, 2)], g_s)
    for one in (table_own, table_far, outw):
        one.close()
    pltpu.make_async_copy(stage, out_ref, out_s).wait()


def body(
    token_ids, embed_table, norm_gain, in_weight, short_filter, long_filter, long_skip, out_weight
):
    tok = token_ids.reshape(8, 128)
    gain = norm_gain.reshape(4, 1, 512)
    w = in_weight.transpose(1, 0, 2)
    short = short_filter.transpose(1, 0, 2)
    skip = long_skip.reshape(1, 512)
    vmem = pl.BlockSpec(memory_space=pltpu.VMEM)
    dma = pltpu.SemaphoreType.DMA
    out = pl.pallas_call(
        kernel,
        out_shape=jax.ShapeDtypeStruct((512, 1024), BF16),
        in_specs=[vmem] * 8,
        out_specs=pl.BlockSpec(memory_space=pl.ANY),
        scratch_shapes=[
            pltpu.VMEM((8, 128), jnp.int32),
            pltpu.VMEM((2, 4, 3, 8, 128), F32),
            pltpu.VMEM((2, 32, 128), F32),
            pltpu.VMEM((LINE, 32, 128), BF16),
            pltpu.VMEM((4, 32, 128), BF16),
            pltpu.VMEM((NX, LINE, 32, 128), BF16),
            pltpu.VMEM((NY, 128, 512), BF16),
            pltpu.VMEM((2, LINE, NX, 96, 128), BF16),
            pltpu.VMEM((LINE, NX, 4, 32, 128), BF16),
            pltpu.VMEM((NY, 4, 128, 1024), BF16),
            pltpu.VMEM((TILES * 128, 512), BF16),
            pltpu.VMEM((2, 32, 256, 128), BF16),
            pltpu.VMEM((2, 4, 128, 8), F32),
            pltpu.VMEM((512, 384), BF16),
            pltpu.VMEM((3, TILES * 128, 128), F32),
            pltpu.VMEM((TILES, 128, 128), BF16),
            pltpu.VMEM((TILES, 128, 128), BF16),
            pltpu.VMEM((512, 1024), F32),
            pltpu.VMEM((512, 1024), BF16),
            dma, dma, dma((2,)), dma((2,)), dma, dma, dma, dma((3, 2)),
            dma((2,)), dma((4,)), dma, dma, dma, dma,
            dma((3,)), dma((5,)), dma((3,)), dma((48,)), dma((3,)), dma((3, 4)), dma, dma((2,)), dma,
        ],
        compiler_params=pltpu.CompilerParams(
            collective_id=0, has_side_effects=True, vmem_limit_bytes=60 * 2**20
        ),
    )(tok, embed_table, gain, w, out_weight.T, short, skip, long_filter)
    return out.T


def solution(mesh):
    placed = (
        P("seq"),
        P(None, "tp"),
        P(),
        P("seq", None, "tp"),
        P(None, None, "tp"),
        P("tp", None),
        P("tp"),
        P("tp", "seq"),
    )
    return jax.shard_map(
        body, mesh=mesh, in_specs=placed, out_specs=P("seq", "tp"), check_vma=False
    )
```

```python
import functools

import jax
import jax.numpy as jnp
from jax import lax
from jax.experimental import pallas as pl
from jax.experimental.pallas import tpu as pltpu
from jax.sharding import PartitionSpec as P

MESH = pl.DeviceIdType.MESH
BF16 = jnp.bfloat16
F32 = jnp.float32
NX, NZ, NC, NY = 4, 8, 2, 4
LINE = NZ * NC
TILES = 10


def kernel(
    tok_ref, emb_ref, gain_ref, w_ref, wo_ref, short_ref, skip_ref, long_ref, out_ref,
    tprev, sf, lf, wsend, wosend, wl, e4, tt, wt, g4, oneh, band, taps, tabn, proj, pt, qt, onet, acc, stage,
    tok_s, tok_r, fil_s, fil_r, s1_s, s1_r, s2_s, s2_r, far_r, e_s, e_r, wo_s, wo_r, t2_s, t2_r,
    ax_s, ax_r, az_s, az_r, ad_s, ad_r, wz_s, wz_r, wx_s, wx_r, wd_s, wd_r, tx_r, td_r, g_s, g_r, out_s,
):
    s = lax.axis_index("seq")
    y = lax.axis_index("tp")
    zc = lax.rem(s, LINE)
    x = s // LINE
    z = zc // NC
    c = lax.rem(zc, NC)
    sign = 1 - 2 * c
    far = lax.rem(y + 2, NY)
    turned = y * LINE + zc

    def at_x(q):
        return (lax.rem(x + q, NX) * LINE + zc, y)

    def at_y(q):
        return (s, lax.rem(y + q, NY))

    def at_z(q):
        return (x * LINE + lax.rem(z + q + NZ, NZ) * NC + c, y)

    mate = (s + sign, y)
    after = (lax.rem(s + 1, NX * LINE), y)
    before = (lax.rem(s + NX * LINE - 1, NX * LINE), y)

    def copy(src, dst, ss, rs, dev):
        return pltpu.make_async_remote_copy(
            src_ref=src, dst_ref=dst, send_sem=ss, recv_sem=rs, device_id=dev, device_id_type=MESH
        )

    def send(*args):
        copy(*args).start()

    def got(ref, rs):
        copy(ref, ref, tok_s, rs, mate).wait_recv()

    def gone(ref, ss):
        copy(ref, ref, ss, tok_r, mate).wait_send()

    hello = pltpu.get_barrier_semaphore()
    greeted = 0
    for r in range(1, LINE):
        pl.semaphore_signal(
            hello, inc=1, device_id=(x * LINE + lax.rem(zc + r, LINE), y), device_id_type=MESH
        )
        greeted += 1
    for r in range(1, NX):
        pl.semaphore_signal(hello, inc=1, device_id=at_x(r), device_id_type=MESH)
        pl.semaphore_signal(hello, inc=1, device_id=at_y(r), device_id_type=MESH)
        greeted += 2
    pl.semaphore_signal(hello, inc=1, device_id=after, device_id_type=MESH)
    pl.semaphore_signal(hello, inc=1, device_id=before, device_id_type=MESH)
    greeted += 2

    @pl.when(x != y)
    def _():
        pl.semaphore_signal(hello, inc=1, device_id=(turned, x), device_id_type=MESH)

    lane32 = lax.broadcasted_iota(jnp.int32, (32, 128), 1) // 32
    for p in range(4):
        chunk = [w_ref[part, :, p * 128 : (p + 1) * 128] for part in range(3)]
        for n in range(4):
            moved = [
                chunk[part] if part == n else pltpu.roll(chunk[part], (part - n) % 4 * 32, 1)
                for part in range(3)
            ]
            wsend[4 * p + n] = jnp.where(
                lane32 == 0, moved[0], jnp.where(lane32 == 1, moved[1], moved[2])
            )
        wosend[p] = wo_ref[:, p * 128 : (p + 1) * 128]
        for part in range(3):
            sf[0, p, part, 0:7, :] = short_ref[part, :, p * 128 : (p + 1) * 128]
            sf[0, p, part, 7:8, :] = skip_ref[:, p * 128 : (p + 1) * 128]
    lf[0] = long_ref[...].astype(F32)
    wl[x, zc] = wsend[zc]
    e4[y] = emb_ref[pl.ds(pl.multiple_of(x * 128, 128), 128), :]

    @pl.when(x == y)
    def _():
        wt[z, c, x] = wosend[...]

    pl.semaphore_wait(hello, greeted + jnp.where(x == y, 0, 1))

    half = pl.ds(pl.multiple_of(64 * c, 64), 64)
    other = pl.ds(pl.multiple_of(64 - 64 * c, 64), 64)
    order = (4, 3, 5, 2, 6, 1, 7, 0)
    for d in order:
        for n in range(NC):
            if d or n:
                to = lax.rem(z + d, NZ) * NC + lax.rem(c + n, NC)
                send(wsend.at[to], wl.at[x, zc], s1_s, s1_r.at[d], (x * LINE + to, y))
    for r in (2, 1, 3):
        send(
            emb_ref.at[pl.ds(pl.multiple_of(x * 128 + 64 * c, 64), 64)],
            e4.at[y, half], e_s.at[0], e_r.at[r - 1], at_y(r),
        )
    send(tok_ref, tprev, tok_s, tok_r, after)
    send(sf.at[0], sf.at[1], fil_s.at[0], fil_r.at[0], at_y(2))
    send(lf.at[0], lf.at[1], fil_s.at[1], fil_r.at[1], at_y(2))

    @pl.when(x != y)
    def _():
        copy(wosend, wt.at[z, c, y], wo_s, wo_r, (turned, x)).start()

    ids = lax.broadcasted_iota(jnp.int32, (128, 512), 1)

    def onehot(tile, column):
        oneh[tile * 128 : (tile + 1) * 128, :] = jnp.where(
            ids == jnp.broadcast_to(column, (128, 512)), 1.0, 0.0
        ).astype(BF16)

    names = tok_ref[...].T
    for tile in range(8):
        onehot(tile + 2, names[:, tile : tile + 1])

    above = lax.broadcasted_iota(jnp.int32, (128, 128), 1) >= lax.broadcasted_iota(
        jnp.int32, (128, 128), 0
    )

    def bands(which, begin, end):
        def build(g, carry):
            rows = jnp.broadcast_to(lf[which, pl.ds(g, 1), :], (128, 128))
            moved = pltpu.roll(rows, 0, 1, stride=1, stride_axis=0)
            band[which, g, 0:128, :] = jnp.where(above, 0.0, moved).astype(BF16)
            band[which, g, 128:256, :] = jnp.where(above, moved, 0.0).astype(BF16)
            return carry

        lax.fori_loop(begin, end, build, 0)

    def columns(which):
        for p in range(4):
            taps[which, p] = sf[which, p, 0].T

    columns(0)
    bands(0, 0, 32)

    def unit(q, d):
        return wl.at[lax.rem(x + q, NX), pl.ds(lax.rem(z + NZ - d, NZ) * NC, NC)]

    def line(d):
        got(unit(0, d) if d else wl.at[x, pl.ds(zc, 1)], s1_r.at[d])
        here = unit(0, d)
        for way, q in ((0, 1), (1, 3)):
            send(here, here, s2_s, s2_r.at[way, d], at_x(q))

    def relay(k):
        d = order[-1 - k]
        for way, q in ((0, 1), (1, 3)):
            here = unit(NX - q, d)
            got(here, s2_r.at[way, d])
            if k % 2 == way:
                send(here, here, s2_s, far_r.at[way], at_x(q))

    for k in range(NZ):
        line(order[-1 - k])
    for k in range(NZ - 2):
        relay(k)
    for r in (1, 3, 2):
        here = e4.at[lax.rem(y + NY - r, NY), half]
        got(here, e_r.at[r - 1])
        send(here, here, e_s.at[1], e_r.at[3], mate)
    relay(NZ - 2)
    relay(NZ - 1)
    got(e4.at[pl.ds(0, 3), other], e_r.at[3])

    total = jnp.zeros((128, 1), F32)
    for k in range(NY):
        piece = e4[k].astype(F32)
        total = total + jnp.sum(piece * piece, axis=1, keepdims=True)
    scale = lax.rsqrt(total * (1.0 / 2048) + 1e-06)
    normed = [
        (e4[k].astype(F32) * scale * gain_ref[k]).astype(BF16) for k in range(NY)
    ]
    got(tprev, tok_r)
    names = jnp.where(s == 0, -1, tprev[...]).T
    for tile in range(2):
        onehot(tile, names[:, tile + 6 : tile + 7])

    for way in range(2):
        got(wl.at[lax.rem(x + 2, NX), pl.ds(0, 8)], far_r.at[way])
    table = jnp.zeros((128, 128), F32)
    for k in range(NX):
        table = table + jnp.dot(
            normed[k], wl[k].reshape(512, 128), preferred_element_type=F32
        )
    tt[0, z, c, x] = table.T[0:96].astype(BF16)

    class Gather:
        def __init__(self, buf):
            self.buf = buf

        def ref(self, hop, step):
            return self.buf.at[lax.rem(z - hop * step + NZ, NZ), c]

        def zsend(self, way, step):
            hop = sign if way == 0 else -sign
            here = self.ref(hop, step - 1)
            send(here, here, az_s, az_r.at[way * 4 + step - 1], at_z(hop))

        def dsend(self, step, here):
            send(here, here, ad_s, ad_r.at[step - 1], mate)

        def xsend(self):
            here = self.buf.at[z, c, x]
            for q in range(1, NX):
                send(here, here, ax_s, ax_r, at_x(q))

        def first(self):
            got(self.buf.at[z, c, pl.ds(0, 3)], ax_r)
            self.zsend(0, 1)
            self.zsend(1, 1)
            self.dsend(1, self.ref(0, 0))

        def step(self, i):
            for way in range(2):
                last = 4 if way == 0 else 3
                if i <= last:
                    here = self.ref(sign if way == 0 else -sign, i)
                    got(here, az_r.at[way * 4 + i - 1])
                    if i < last:
                        self.zsend(way, i + 1)
                    self.dsend(i, here)

        def settle(self, i):
            got(self.buf.at[pl.ds(0, (3, 2, 2, 1)[i - 1]), 0], ad_r.at[i - 1])

        def close(self):
            gone(self.buf.at[0, 0, pl.ds(0, 3)], ax_s)
            gone(self.buf.at[pl.ds(0, 7), 0], az_s)
            gone(self.buf.at[:, 0], ad_s)

    class Spread:
        def __init__(self, n, buf):
            self.n, self.buf = n, buf

        def onward(self, way, step):
            hop = sign if way == 0 else -sign
            here = self.buf.at[lax.rem(z - hop * step + NZ, NZ), c, x]
            if step:
                got(here, wz_r.at[self.n, way * 4 + step - 1])
            if step < (4 if way == 0 else 3):
                send(here, here, wz_s.at[self.n], wz_r.at[self.n, way * 4 + step], at_z(hop))
            if step or way == 0:
                arrive = tx_r.at[step] if self.n == 0 else wx_r
                for q in (2, 1, 3):
                    send(here, here, wx_s.at[self.n], arrive, at_x(q))

        def step(self, i):
            self.onward(0, i)
            if i < 4:
                self.onward(1, i)

        def across(self, i):
            hops = ((0,), (sign, -sign), (sign, -sign), (sign, -sign), (sign,))[i]
            got(self.buf.at[pl.ds(0, len(hops)), 0, pl.ds(0, 3)], tx_r.at[i])
            for hop in hops:
                here = self.buf.at[lax.rem(z - hop * i + NZ, NZ), c]
                send(here, here, wd_s.at[0], td_r.at[max(i, 1) - 1], mate)

        def settle(self, i):
            got(self.buf.at[pl.ds(0, (3, 2, 2, 1)[i - 1]), 0], td_r.at[i - 1])

        def share(self):
            got(self.buf.at[pl.ds(0, 3)], wx_r)
            here = self.buf.at[:, c]
            send(here, here, wd_s.at[1], wd_r, mate)

        def shared(self):
            got(self.buf.at[:, 1 - c], wd_r)

        def close(self):
            gone(self.buf.at[pl.ds(0, 7), 0, 0], wz_s.at[self.n])
            gone(self.buf.at[pl.ds(0, 3)], wx_s.at[self.n])
            gone(self.buf.at[:, c], wd_s.at[self.n])

    table_own = Spread(0, tt.at[0])
    table_far = Gather(tt.at[1])
    outw = Spread(1, wt)

    table_own.step(0)
    send(tt.at[0, z, c, x], tt.at[1, z, c, x], t2_s, t2_r, at_y(2))
    got(sf.at[1], fil_r.at[0])
    got(lf.at[1], fil_r.at[1])
    columns(1)
    bands(1, 0, 16)
    table_own.step(1)
    bands(1, 16, 24)
    table_own.step(2)
    bands(1, 24, 32)
    got(tt.at[1, z, c, x], t2_r)
    table_far.xsend()

    @pl.when(x != y)
    def _():
        copy(wosend, wt.at[z, c, x], wo_s, wo_r, mate).wait()

    table_own.across(0)
    table_own.across(1)

    pair0 = z // 2
    even = 1 - 2 * lax.rem(z, 2)

    def pair(i):
        move = (0, -even, even, 2)[i - 1]
        return lax.rem(pair0 + move + 4, 4)

    def block(which, k, p, early=None, late=None):
        table = jnp.concatenate(
            [
                jnp.concatenate(
                    [
                        tt[which, 2 * p + n // 2, n % 2, b, part * 32 : (part + 1) * 32, :]
                        for part in range(3)
                        for n in range(4)
                    ],
                    axis=0,
                )
                for b in range(NX)
            ],
            axis=1,
        )
        tabn[...] = table.T
        for n in range(5):
            rows = slice(n * 256, (n + 1) * 256)
            both = jnp.dot(oneh[rows, :], tabn[...], preferred_element_type=F32)
            for part in range(3):
                proj[part, rows, :] = both[:, part * 128 : (part + 1) * 128]

        if early:
            early()

        def fir(part, row, count):
            total = None
            for lag in range(7):
                tap = jnp.broadcast_to(sf[which, p, part, lag : lag + 1, :], (count, 128))
                term = tap * proj[part, pl.ds(row - lag, count), :]
                total = term if total is None else total + term
            return total

        def tile(n, carry):
            row = pl.multiple_of(n * 128, 128)
            prod, query = [], []
            for h in range(4):
                prod.append((fir(1, row + 32 * h, 32) * fir(2, row + 32 * h, 32)).astype(BF16))
                query.append(fir(0, row + 32 * h, 32).astype(BF16))
            pt[n] = jnp.concatenate(prod, axis=0).T
            qt[n] = jnp.concatenate(query, axis=0).T
            return carry

        lax.fori_loop(1, TILES, tile, 0)
        if late:
            late()

        def groups(h, carry):
            for n in range(4):
                g = 4 * h + n
                ch = pl.ds(pl.multiple_of(g * 16, 16), 16)
                prod = [pt[t, ch, :] for t in range(1, TILES)]
                rows = jnp.concatenate(
                    [jnp.concatenate([prod[t], prod[t + 1]], axis=1) for t in range(8)], axis=0
                )
                conv = jnp.dot(rows, band[which, 8 * p + g], preferred_element_type=F32).astype(BF16)
                skip = jnp.broadcast_to(taps[which, p, ch, 7:8], (16, 128)).astype(BF16)
                for t in range(8):
                    whole = conv[t * 16 : (t + 1) * 16] + skip * prod[t + 1]
                    g4[k, p, ch, t * 128 : (t + 1) * 128] = qt[t + 2, ch, :] * whole
            return carry

        lax.fori_loop(0, 2, groups, 0)

    def gsend(i):
        here = g4.at[y, pair(i)]
        for way, q in ((0, 1), (1, 3)):
            send(here, here, g_s, g_r.at[way], at_y(q))

    def own(i, **hooks):
        table_own.settle(i)
        block(0, y, pair(i), **hooks)
        gsend(i)

    def others(i, **hooks):
        table_far.settle(i)
        block(1, far, pair(i), **hooks)

    def resid():
        below = lax.broadcasted_iota(jnp.int32, (512, 128), 0)
        for n in range(8):
            row = tok_ref[n : n + 1, :]
            onet[:, n * 128 : (n + 1) * 128] = jnp.where(below == row, 1.0, 0.0).astype(BF16)
        for n in range(4):
            cols = slice(n * 128, (n + 1) * 128)
            acc[cols, :] = jnp.dot(emb_ref[:, cols].T, onet[...], preferred_element_type=F32)

    def after1():
        table_own.step(3)
        table_own.across(2)
        table_far.first()

    def after2():
        table_own.step(4)
        table_own.across(3)
        outw.step(0)

    def after3():
        table_own.across(4)
        table_far.step(1)
        outw.step(1)

    def after4():
        table_far.step(2)
        outw.step(2)

    def after5():
        table_far.step(3)
        outw.step(3)

    def after6():
        table_far.step(4)
        outw.step(4)

    own(1, late=after1)
    resid()
    own(2, early=after2)
    own(3, early=after3)
    own(4, early=after4)
    others(1, early=after5)
    others(2, early=after6)
    others(3)
    others(4, early=outw.share)
    outw.shared()

    def project(ks, n):
        sums = None
        for k in ks:
            left = jnp.concatenate(
                [wt[pl.ds(2 * n, 2), :, k, p].reshape(128, 128) for p in range(4)], axis=1
            )
            term = jnp.dot(left, g4[k].reshape(512, 1024), preferred_element_type=F32)
            sums = term if sums is None else sums + term
        return sums

    def near(n, carry):
        cols = pl.ds(pl.multiple_of(n * 128, 128), 128)
        acc[cols, :] = acc[cols, :] + project((y, far), n)
        return carry

    lax.fori_loop(0, 4, near, 0)
    for way, q in ((0, 3), (1, 1)):
        got(g4.at[lax.rem(y + q, NY)], g_r.at[way])

    def rest(n, carry):
        rows = pl.ds(pl.multiple_of(n * 128, 128), 128)
        ks = (lax.rem(y + 1, NY), lax.rem(y + 3, NY))
        stage[rows, :] = (acc[rows, :] + project(ks, n)).astype(BF16)
        pltpu.make_async_copy(stage.at[rows], out_ref.at[rows], out_s).start()
        return carry

    lax.fori_loop(0, 4, rest, 0)
    gone(wsend.at[pl.ds(0, LINE - 1)], s1_s)
    gone(wl.at[pl.ds(0, 3)], s2_s)
    for n in range(2):
        gone(e4.at[pl.ds(0, 3), half], e_s.at[n])
        gone((sf, lf)[n].at[0], fil_s.at[n])
    gone(tok_ref, tok_s)
    gone(tt.at[0, z, c, x], t2_s)
    gone(g4.at[pl.ds(0, 2)], g_s)
    for one in (table_own, table_far, outw):
        one.close()
    pltpu.make_async_copy(stage, out_ref, out_s).wait()


def body(
    token_ids, embed_table, norm_gain, in_weight, short_filter, long_filter, long_skip, out_weight
):
    tok = token_ids.reshape(8, 128)
    gain = norm_gain.reshape(4, 1, 512)
    w = in_weight.transpose(1, 0, 2)
    short = short_filter.transpose(1, 0, 2)
    skip = long_skip.reshape(1, 512)
    vmem = pl.BlockSpec(memory_space=pltpu.VMEM)
    dma = pltpu.SemaphoreType.DMA
    out = pl.pallas_call(
        kernel,
        out_shape=jax.ShapeDtypeStruct((512, 1024), BF16),
        in_specs=[vmem] * 8,
        out_specs=pl.BlockSpec(memory_space=pl.ANY),
        scratch_shapes=[
            pltpu.VMEM((8, 128), jnp.int32),
            pltpu.VMEM((2, 4, 3, 8, 128), F32),
            pltpu.VMEM((2, 32, 128), F32),
            pltpu.VMEM((LINE, 32, 128), BF16),
            pltpu.VMEM((4, 32, 128), BF16),
            pltpu.VMEM((NX, LINE, 32, 128), BF16),
            pltpu.VMEM((NY, 128, 512), BF16),
            pltpu.VMEM((2, NZ, NC, NX, 96, 128), BF16),
            pltpu.VMEM((NZ, NC, NX, 4, 32, 128), BF16),
            pltpu.VMEM((NY, 4, 128, 1024), BF16),
            pltpu.VMEM((TILES * 128, 512), BF16),
            pltpu.VMEM((2, 32, 256, 128), BF16),
            pltpu.VMEM((2, 4, 128, 8), F32),
            pltpu.VMEM((512, 384), BF16),
            pltpu.VMEM((3, TILES * 128, 128), F32),
            pltpu.VMEM((TILES, 128, 128), BF16),
            pltpu.VMEM((TILES, 128, 128), BF16),
            pltpu.VMEM((512, 1024), BF16),
            pltpu.VMEM((512, 1024), F32),
            pltpu.VMEM((512, 1024), BF16),
            dma, dma, dma((2,)), dma((2,)), dma, dma((8,)), dma, dma((2, 8)), dma((2,)),
            dma((2,)), dma((4,)), dma, dma, dma, dma,
            dma, dma, dma, dma((8,)), dma, dma((4,)),
            dma((2,)), dma((2, 8)), dma((2,)), dma, dma((2,)), dma, dma((5,)), dma((4,)),
            dma, dma((2,)), dma,
        ],
        compiler_params=pltpu.CompilerParams(
            collective_id=0, has_side_effects=True, vmem_limit_bytes=60 * 2**20
        ),
    )(tok, embed_table, gain, w, out_weight.T, short, skip, long_filter)
    return out.T


def solution(mesh):
    placed = (
        P("seq"),
        P(None, "tp"),
        P(),
        P("seq", None, "tp"),
        P(None, None, "tp"),
        P("tp", None),
        P("tp"),
        P("tp", "seq"),
    )
    return jax.shard_map(
        body, mesh=mesh, in_specs=placed, out_specs=P("seq", "tp"), check_vma=False
    )
```

```python
import functools

import jax
import jax.numpy as jnp
from jax import lax
from jax.experimental import pallas as pl
from jax.experimental.pallas import tpu as pltpu
from jax.sharding import PartitionSpec as P

MESH = pl.DeviceIdType.MESH
BF16 = jnp.bfloat16
F32 = jnp.float32
NX, NZ, NC, NY = 4, 8, 2, 4
LINE = NZ * NC
ROWS = 16 + 9 * 128


def kernel(
    tok_in, emb_in, gain_in, w_in, wo_in, short_in, skip_in, long_in, out_ref,
    tok_ref, emb_ref, gain_ref, w_ref, wo_ref, short_ref, skip_ref, long_ref, in_s, tprev, sf, lf, wsend, wosend, wl, e4, tt, wt, g4, oneh, band, taps, tabn, proj, pt, qt, onet, acc, stage,
    tok_s, tok_r, fil_s, fil_r, s1_s, s1_r, s2_s, s2_r, far_r, e_s, e_r, wo_s, wo_r, t2_s, t2_r,
    ax_s, ax_r, az_s, az_r, ad_s, ad_r, wz_s, wz_r, wx_s, wx_r, wd_s, wd_r, tx_r, td_r, g_s, g_r, out_s,
):
    s = lax.axis_index("seq")
    y = lax.axis_index("tp")
    zc = lax.rem(s, LINE)
    x = s // LINE
    z = zc // NC
    c = lax.rem(zc, NC)
    sign = 1 - 2 * c
    far = lax.rem(y + 2, NY)
    turned = y * LINE + zc

    def at_x(q):
        return (lax.rem(x + q, NX) * LINE + zc, y)

    def at_y(q):
        return (s, lax.rem(y + q, NY))

    def at_z(q):
        return (x * LINE + lax.rem(z + q + NZ, NZ) * NC + c, y)

    mate = (s + sign, y)
    after = (lax.rem(s + 1, NX * LINE), y)
    before = (lax.rem(s + NX * LINE - 1, NX * LINE), y)

    def copy(src, dst, ss, rs, dev):
        return pltpu.make_async_remote_copy(
            src_ref=src, dst_ref=dst, send_sem=ss, recv_sem=rs, device_id=dev, device_id_type=MESH
        )

    def send(*args):
        copy(*args).start()

    def got(ref, rs):
        copy(ref, ref, tok_s, rs, mate).wait_recv()

    def gone(ref, ss):
        copy(ref, ref, ss, tok_r, mate).wait_send()

    inputs = [
        pltpu.make_async_copy(src, dst, in_s.at[n])
        for n, (src, dst) in enumerate(
            [
                (w_in, w_ref), (wo_in, wo_ref), (short_in, short_ref), (skip_in, skip_ref),
                (long_in, long_ref), (tok_in, tok_ref), (emb_in, emb_ref), (gain_in, gain_ref),
            ]
        )
    ]

    hello = pltpu.get_barrier_semaphore()
    greeted = 0
    for r in range(1, LINE):
        pl.semaphore_signal(
            hello, inc=1, device_id=(x * LINE + lax.rem(zc + r, LINE), y), device_id_type=MESH
        )
        greeted += 1
    for r in range(1, NX):
        pl.semaphore_signal(hello, inc=1, device_id=at_x(r), device_id_type=MESH)
        pl.semaphore_signal(hello, inc=1, device_id=at_y(r), device_id_type=MESH)
        greeted += 2
    pl.semaphore_signal(hello, inc=1, device_id=after, device_id_type=MESH)
    pl.semaphore_signal(hello, inc=1, device_id=before, device_id_type=MESH)
    greeted += 2

    @pl.when(x != y)
    def _():
        pl.semaphore_signal(hello, inc=1, device_id=(turned, x), device_id_type=MESH)

    for one in inputs:
        one.start()
    for one in inputs:
        one.wait()
    lane32 = lax.broadcasted_iota(jnp.int32, (32, 128), 1) // 32
    for p in range(4):
        chunk = [w_ref[part, :, p * 128 : (p + 1) * 128] for part in range(3)]
        for n in range(4):
            moved = [
                chunk[part] if part == n else pltpu.roll(chunk[part], (part - n) % 4 * 32, 1)
                for part in range(3)
            ]
            wsend[4 * p + n] = jnp.where(
                lane32 == 0, moved[0], jnp.where(lane32 == 1, moved[1], moved[2])
            )
        wosend[p] = wo_ref[:, p * 128 : (p + 1) * 128]
        for part in range(3):
            sf[0, p, part, 0:7, :] = short_ref[part, :, p * 128 : (p + 1) * 128]
            sf[0, p, part, 7:8, :] = skip_ref[:, p * 128 : (p + 1) * 128]
    lf[0] = long_ref[...].astype(F32)
    wl[x, zc] = wsend[zc]
    e4[y] = emb_ref[pl.ds(pl.multiple_of(x * 128, 128), 128), :]

    @pl.when(x == y)
    def _():
        wt[z, c, x] = wosend[...]

    pl.semaphore_wait(hello, greeted + jnp.where(x == y, 0, 1))

    half = pl.ds(pl.multiple_of(64 * c, 64), 64)
    other = pl.ds(pl.multiple_of(64 - 64 * c, 64), 64)
    order = (4, 3, 5, 2, 6, 1, 7, 0)
    for d in order:
        for n in range(NC):
            if d or n:
                to = lax.rem(z + d, NZ) * NC + lax.rem(c + n, NC)
                send(wsend.at[to], wl.at[x, zc], s1_s, s1_r.at[d], (x * LINE + to, y))
    for r in (2, 1, 3):
        send(
            emb_ref.at[pl.ds(pl.multiple_of(x * 128 + 64 * c, 64), 64)],
            e4.at[y, half], e_s.at[0], e_r.at[r - 1], at_y(r),
        )
    send(tok_ref, tprev, tok_s, tok_r, after)
    send(sf.at[0], sf.at[1], fil_s.at[0], fil_r.at[0], at_y(2))
    send(lf.at[0], lf.at[1], fil_s.at[1], fil_r.at[1], at_y(2))

    @pl.when(x != y)
    def _():
        copy(wosend, wt.at[z, c, y], wo_s, wo_r, (turned, x)).start()

    ids = lax.broadcasted_iota(jnp.int32, (128, 512), 1)

    def onehot(begin, column):
        size = column.shape[0]
        oneh[begin : begin + size, :] = jnp.where(
            ids[:size] == jnp.broadcast_to(column, (size, 512)), 1.0, 0.0
        ).astype(BF16)

    names = tok_ref[...].T
    for tile in range(8):
        onehot(144 + tile * 128, names[:, tile : tile + 1])

    above = lax.broadcasted_iota(jnp.int32, (128, 128), 1) >= lax.broadcasted_iota(
        jnp.int32, (128, 128), 0
    )

    def bands(which, begin, end):
        def build(g, carry):
            rows = jnp.broadcast_to(lf[which, pl.ds(g, 1), :], (128, 128))
            moved = pltpu.roll(rows, 0, 1, stride=1, stride_axis=0)
            band[which, g, 0:128, :] = jnp.where(above, 0.0, moved).astype(BF16)
            band[which, g, 128:256, :] = jnp.where(above, moved, 0.0).astype(BF16)
            return carry

        lax.fori_loop(begin, end, build, 0)

    def columns(which):
        for p in range(4):
            taps[which, p] = sf[which, p, 0].T

    columns(0)
    bands(0, 0, 32)

    def unit(q, d):
        return wl.at[lax.rem(x + q, NX), pl.ds(lax.rem(z + NZ - d, NZ) * NC, NC)]

    def line(d):
        got(unit(0, d) if d else wl.at[x, pl.ds(zc, 1)], s1_r.at[d])
        here = unit(0, d)
        for way, q in ((0, 1), (1, 3)):
            send(here, here, s2_s, s2_r.at[way, d], at_x(q))

    def relay(k):
        d = order[-1 - k]
        for way, q in ((0, 1), (1, 3)):
            here = unit(NX - q, d)
            got(here, s2_r.at[way, d])
            if k % 2 == way:
                send(here, here, s2_s, far_r.at[way], at_x(q))

    for k in range(NZ):
        line(order[-1 - k])
    for k in range(NZ - 2):
        relay(k)
    for r in (1, 3, 2):
        here = e4.at[lax.rem(y + NY - r, NY), half]
        got(here, e_r.at[r - 1])
        send(here, here, e_s.at[1], e_r.at[3], mate)
    relay(NZ - 2)
    relay(NZ - 1)
    got(e4.at[pl.ds(0, 3), other], e_r.at[3])

    total = jnp.zeros((128, 1), F32)
    for k in range(NY):
        piece = e4[k].astype(F32)
        total = total + jnp.sum(piece * piece, axis=1, keepdims=True)
    scale = lax.rsqrt(total * (1.0 / 2048) + 1e-06)
    normed = [
        (e4[k].astype(F32) * scale * gain_ref[k]).astype(BF16) for k in range(NY)
    ]
    got(tprev, tok_r)
    names = jnp.where(s == 0, -1, tprev[...]).T
    onehot(0, names[112:128, 6:7])
    onehot(16, names[:, 7:8])

    for way in range(2):
        got(wl.at[lax.rem(x + 2, NX), pl.ds(0, 8)], far_r.at[way])
    table = jnp.zeros((128, 128), F32)
    for k in range(NX):
        table = table + jnp.dot(
            normed[k], wl[k].reshape(512, 128), preferred_element_type=F32
        )
    tt[0, z, c, x] = table.T[0:96].astype(BF16)

    class Gather:
        def __init__(self, buf):
            self.buf = buf

        def ref(self, hop, step):
            return self.buf.at[lax.rem(z - hop * step + NZ, NZ), c]

        def zsend(self, way, step):
            hop = sign if way == 0 else -sign
            here = self.ref(hop, step - 1)
            send(here, here, az_s, az_r.at[way * 4 + step - 1], at_z(hop))

        def dsend(self, step, here):
            send(here, here, ad_s, ad_r.at[step - 1], mate)

        def xsend(self):
            here = self.buf.at[z, c, x]
            for q in range(1, NX):
                send(here, here, ax_s, ax_r, at_x(q))

        def first(self):
            got(self.buf.at[z, c, pl.ds(0, 3)], ax_r)
            self.zsend(0, 1)
            self.zsend(1, 1)
            self.dsend(1, self.ref(0, 0))

        def step(self, i):
            for way in range(2):
                last = 4 if way == 0 else 3
                if i <= last:
                    here = self.ref(sign if way == 0 else -sign, i)
                    got(here, az_r.at[way * 4 + i - 1])
                    if i < last:
                        self.zsend(way, i + 1)
                    self.dsend(i, here)

        def settle(self, i):
            got(self.buf.at[pl.ds(0, (3, 2, 2, 1)[i - 1]), 0], ad_r.at[i - 1])

        def close(self):
            gone(self.buf.at[0, 0, pl.ds(0, 3)], ax_s)
            gone(self.buf.at[pl.ds(0, 7), 0], az_s)
            gone(self.buf.at[:, 0], ad_s)

    class Spread:
        def __init__(self, n, buf):
            self.n, self.buf = n, buf

        def onward(self, way, step):
            hop = sign if way == 0 else -sign
            here = self.buf.at[lax.rem(z - hop * step + NZ, NZ), c, x]
            if step:
                got(here, wz_r.at[self.n, way * 4 + step - 1])
            if step < (4 if way == 0 else 3):
                send(here, here, wz_s.at[self.n], wz_r.at[self.n, way * 4 + step], at_z(hop))
            if step or way == 0:
                arrive = tx_r.at[step] if self.n == 0 else wx_r
                for q in (2, 1, 3):
                    send(here, here, wx_s.at[self.n], arrive, at_x(q))

        def step(self, i):
            self.onward(0, i)
            if i < 4:
                self.onward(1, i)

        def across(self, i):
            hops = ((0,), (sign, -sign), (sign, -sign), (sign, -sign), (sign,))[i]
            got(self.buf.at[pl.ds(0, len(hops)), 0, pl.ds(0, 3)], tx_r.at[i])
            for hop in hops:
                here = self.buf.at[lax.rem(z - hop * i + NZ, NZ), c]
                send(here, here, wd_s.at[0], td_r.at[max(i, 1) - 1], mate)

        def settle(self, i):
            got(self.buf.at[pl.ds(0, (3, 2, 2, 1)[i - 1]), 0], td_r.at[i - 1])

        def share(self):
            got(self.buf.at[pl.ds(0, 3)], wx_r)
            here = self.buf.at[:, c]
            send(here, here, wd_s.at[1], wd_r, mate)

        def shared(self):
            got(self.buf.at[:, 1 - c], wd_r)

        def close(self):
            gone(self.buf.at[pl.ds(0, 7), 0, 0], wz_s.at[self.n])
            gone(self.buf.at[pl.ds(0, 3)], wx_s.at[self.n])
            gone(self.buf.at[:, c], wd_s.at[self.n])

    table_own = Spread(0, tt.at[0])
    table_far = Gather(tt.at[1])
    outw = Spread(1, wt)

    table_own.step(0)
    send(tt.at[0, z, c, x], tt.at[1, z, c, x], t2_s, t2_r, at_y(2))
    got(sf.at[1], fil_r.at[0])
    got(lf.at[1], fil_r.at[1])
    columns(1)
    bands(1, 0, 16)
    table_own.step(1)
    bands(1, 16, 24)
    table_own.step(2)
    bands(1, 24, 32)
    got(tt.at[1, z, c, x], t2_r)
    table_far.xsend()

    @pl.when(x != y)
    def _():
        copy(wosend, wt.at[z, c, x], wo_s, wo_r, mate).wait()

    table_own.across(0)
    table_own.across(1)

    pair0 = z // 2
    even = 1 - 2 * lax.rem(z, 2)

    def pair(i):
        move = (0, -even, even, 2)[i - 1]
        return lax.rem(pair0 + move + 4, 4)

    def block(which, k, p, early=None, late=None):
        table = jnp.concatenate(
            [
                jnp.concatenate(
                    [
                        tt[which, 2 * p + n // 2, n % 2, b, part * 32 : (part + 1) * 32, :]
                        for part in range(3)
                        for n in range(4)
                    ],
                    axis=0,
                )
                for b in range(NX)
            ],
            axis=1,
        )
        tabn[...] = table.T
        for begin, end in ((0, 304), (304, 592), (592, 880), (880, 1168)):
            rows = slice(begin, end)
            both = jnp.dot(oneh[rows, :], tabn[...], preferred_element_type=F32)
            for part in range(3):
                proj[part, rows, :] = both[:, part * 128 : (part + 1) * 128]

        if early:
            early()

        def fir(part, row, count):
            total = None
            for lag in range(7):
                tap = jnp.broadcast_to(sf[which, p, part, lag : lag + 1, :], (count, 128))
                term = tap * proj[part, pl.ds(row - lag, count), :]
                total = term if total is None else total + term
            return total

        def tile(n, query):
            row = pl.multiple_of(n * 128 + 16, 16)
            pieces = [
                (fir(1, row + 32 * h, 32) * fir(2, row + 32 * h, 32)).astype(BF16) for h in range(4)
            ]
            pt[n] = jnp.concatenate(pieces, axis=0).T
            if query:
                pieces = [fir(0, row + 32 * h, 32).astype(BF16) for h in range(4)]
                qt[n] = jnp.concatenate(pieces, axis=0).T

        def tiles(n, carry):
            tile(n, True)
            return carry

        tile(0, False)
        lax.fori_loop(1, 9, tiles, 0)
        if late:
            late()

        def groups(h, carry):
            for n in range(4):
                g = 4 * h + n
                ch = pl.ds(pl.multiple_of(g * 16, 16), 16)
                prod = [pt[t, ch, :] for t in range(9)]
                rows = jnp.concatenate(
                    [jnp.concatenate([prod[t], prod[t + 1]], axis=1) for t in range(8)], axis=0
                )
                conv = jnp.dot(rows, band[which, 8 * p + g], preferred_element_type=F32).astype(BF16)
                skip = jnp.broadcast_to(taps[which, p, ch, 7:8], (16, 128)).astype(BF16)
                for t in range(8):
                    whole = conv[t * 16 : (t + 1) * 16] + skip * prod[t + 1]
                    g4[k, p, ch, t * 128 : (t + 1) * 128] = qt[t + 1, ch, :] * whole
            return carry

        lax.fori_loop(0, 2, groups, 0)

    def gsend(i):
        here = g4.at[y, pair(i)]
        for way, q in ((0, 1), (1, 3)):
            send(here, here, g_s, g_r.at[way], at_y(q))

    def own(i, **hooks):
        table_own.settle(i)
        block(0, y, pair(i), **hooks)
        gsend(i)

    def others(i, **hooks):
        table_far.settle(i)
        block(1, far, pair(i), **hooks)

    def resid():
        below = lax.broadcasted_iota(jnp.int32, (512, 128), 0)
        for n in range(8):
            row = tok_ref[n : n + 1, :]
            onet[:, n * 128 : (n + 1) * 128] = jnp.where(below == row, 1.0, 0.0).astype(BF16)
        for n in range(4):
            cols = slice(n * 128, (n + 1) * 128)
            acc[cols, :] = jnp.dot(emb_ref[:, cols].T, onet[...], preferred_element_type=F32)

    def late1():
        table_own.step(3)
        table_own.across(2)
        table_far.first()

    def early2():
        table_own.step(4)
        table_own.across(3)
        outw.step(0)

    def early3():
        table_own.across(4)
        outw.step(1)

    own(1, late=late1)
    resid()
    own(2, early=early2, late=lambda: table_far.step(1))
    own(3, early=early3, late=lambda: table_far.step(2))
    own(4, early=lambda: outw.step(2), late=lambda: table_far.step(3))
    others(1, early=lambda: outw.step(3), late=lambda: table_far.step(4))
    others(2, early=lambda: outw.step(4))
    others(3)
    others(4, early=outw.share)
    outw.shared()

    def project(ks, n):
        sums = None
        for k in ks:
            left = jnp.concatenate(
                [wt[pl.ds(2 * n, 2), :, k, p].reshape(128, 128) for p in range(4)], axis=1
            )
            term = jnp.dot(left, g4[k].reshape(512, 1024), preferred_element_type=F32)
            sums = term if sums is None else sums + term
        return sums

    def near(n, carry):
        cols = pl.ds(pl.multiple_of(n * 128, 128), 128)
        acc[cols, :] = acc[cols, :] + project((y, far), n)
        return carry

    lax.fori_loop(0, 4, near, 0)
    for way, q in ((0, 3), (1, 1)):
        got(g4.at[lax.rem(y + q, NY)], g_r.at[way])

    def rest(n, carry):
        rows = pl.ds(pl.multiple_of(n * 128, 128), 128)
        ks = (lax.rem(y + 1, NY), lax.rem(y + 3, NY))
        stage[rows, :] = (acc[rows, :] + project(ks, n)).astype(BF16)
        pltpu.make_async_copy(stage.at[rows], out_ref.at[rows], out_s).start()
        return carry

    lax.fori_loop(0, 4, rest, 0)
    gone(wsend.at[pl.ds(0, LINE - 1)], s1_s)
    gone(wl.at[pl.ds(0, 3)], s2_s)
    for n in range(2):
        gone(e4.at[pl.ds(0, 3), half], e_s.at[n])
        gone((sf, lf)[n].at[0], fil_s.at[n])
    gone(tok_ref, tok_s)
    gone(tt.at[0, z, c, x], t2_s)
    gone(g4.at[pl.ds(0, 2)], g_s)
    for one in (table_own, table_far, outw):
        one.close()
    pltpu.make_async_copy(stage, out_ref, out_s).wait()


def body(
    token_ids, embed_table, norm_gain, in_weight, short_filter, long_filter, long_skip, out_weight
):
    tok = token_ids.reshape(8, 128)
    gain = norm_gain.reshape(4, 1, 512)
    w = in_weight.transpose(1, 0, 2)
    short = short_filter.transpose(1, 0, 2)
    skip = long_skip.reshape(1, 512)
    dma = pltpu.SemaphoreType.DMA
    out = pl.pallas_call(
        kernel,
        out_shape=jax.ShapeDtypeStruct((512, 1024), BF16),
        in_specs=[pl.BlockSpec(memory_space=pl.ANY)] * 8,
        out_specs=pl.BlockSpec(memory_space=pl.ANY),
        scratch_shapes=[
            pltpu.VMEM((8, 128), jnp.int32),
            pltpu.VMEM((512, 512), BF16),
            pltpu.VMEM((4, 1, 512), F32),
            pltpu.VMEM((3, 32, 512), BF16),
            pltpu.VMEM((32, 512), BF16),
            pltpu.VMEM((3, 7, 512), F32),
            pltpu.VMEM((1, 512), F32),
            pltpu.VMEM((32, 128), BF16),
            dma((8,)),
            pltpu.VMEM((8, 128), jnp.int32),
            pltpu.VMEM((2, 4, 3, 8, 128), F32),
            pltpu.VMEM((2, 32, 128), F32),
            pltpu.VMEM((LINE, 32, 128), BF16),
            pltpu.VMEM((4, 32, 128), BF16),
            pltpu.VMEM((NX, LINE, 32, 128), BF16),
            pltpu.VMEM((NY, 128, 512), BF16),
            pltpu.VMEM((2, NZ, NC, NX, 96, 128), BF16),
            pltpu.VMEM((NZ, NC, NX, 4, 32, 128), BF16),
            pltpu.VMEM((NY, 4, 128, 1024), BF16),
            pltpu.VMEM((ROWS, 512), BF16),
            pltpu.VMEM((2, 32, 256, 128), BF16),
            pltpu.VMEM((2, 4, 128, 8), F32),
            pltpu.VMEM((512, 384), BF16),
            pltpu.VMEM((3, ROWS, 128), F32),
            pltpu.VMEM((9, 128, 128), BF16),
            pltpu.VMEM((9, 128, 128), BF16),
            pltpu.VMEM((512, 1024), BF16),
            pltpu.VMEM((512, 1024), F32),
            pltpu.VMEM((512, 1024), BF16),
            dma, dma, dma((2,)), dma((2,)), dma, dma((8,)), dma, dma((2, 8)), dma((2,)),
            dma((2,)), dma((4,)), dma, dma, dma, dma,
            dma, dma, dma, dma((8,)), dma, dma((4,)),
            dma((2,)), dma((2, 8)), dma((2,)), dma, dma((2,)), dma, dma((5,)), dma((4,)),
            dma, dma((2,)), dma,
        ],
        compiler_params=pltpu.CompilerParams(
            collective_id=0, has_side_effects=True, vmem_limit_bytes=60 * 2**20
        ),
    )(tok, embed_table, gain, w, out_weight.T, short, skip, long_filter)
    return out.T


def solution(mesh):
    placed = (
        P("seq"),
        P(None, "tp"),
        P(),
        P("seq", None, "tp"),
        P(None, None, "tp"),
        P("tp", None),
        P("tp"),
        P("tp", "seq"),
    )
    return jax.shard_map(
        body, mesh=mesh, in_specs=placed, out_specs=P("seq", "tp"), check_vma=False
    )
```

```python
import functools

import jax
import jax.numpy as jnp
from jax import lax
from jax.experimental import pallas as pl
from jax.experimental.pallas import tpu as pltpu
from jax.sharding import PartitionSpec as P

MESH = pl.DeviceIdType.MESH
BF16 = jnp.bfloat16
F32 = jnp.float32
NX, NZ, NC, NY = 4, 8, 2, 4
LINE = NZ * NC
ROWS = 16 + 9 * 128


def kernel(
    tok_in, emb_in, gain_in, w_in, wo_in, short_in, skip_in, long_in, out_ref,
    tok_ref, emb_ref, gain_ref, w_ref, wo_ref, short_ref, skip_ref, long_ref, in_s, tprev, sf, lf, wsend, wosend, wl, e4, tt, wt, g4, oneh, band, taps, tabn, proj, pt, qt, onet, acc, stage,
    tok_s, tok_r, fil_s, fil_r, s1_s, s1_r, s2_s, s2_r, far_r, e_s, e_r, wo_s, wo_r, t2_s, t2_r,
    ax_s, ax_r, az_s, az_r, ad_s, ad_r, wz_s, wz_r, wx_s, wx_r, wd_s, wd_r, tx_r, td_r, g_s, g_r, out_s,
):
    s = lax.axis_index("seq")
    y = lax.axis_index("tp")
    zc = lax.rem(s, LINE)
    x = s // LINE
    z = zc // NC
    c = lax.rem(zc, NC)
    sign = 1 - 2 * c
    far = lax.rem(y + 2, NY)
    turned = y * LINE + zc

    def at_x(q):
        return (lax.rem(x + q, NX) * LINE + zc, y)

    def at_y(q):
        return (s, lax.rem(y + q, NY))

    def at_z(q):
        return (x * LINE + lax.rem(z + q + NZ, NZ) * NC + c, y)

    mate = (s + sign, y)
    after = (lax.rem(s + 1, NX * LINE), y)
    before = (lax.rem(s + NX * LINE - 1, NX * LINE), y)

    def copy(src, dst, ss, rs, dev):
        return pltpu.make_async_remote_copy(
            src_ref=src, dst_ref=dst, send_sem=ss, recv_sem=rs, device_id=dev, device_id_type=MESH
        )

    def send(*args):
        copy(*args).start()

    def got(ref, rs):
        copy(ref, ref, tok_s, rs, mate).wait_recv()

    def gone(ref, ss):
        copy(ref, ref, ss, tok_r, mate).wait_send()

    inputs = [
        pltpu.make_async_copy(src, dst, in_s.at[n])
        for n, (src, dst) in enumerate(
            [
                (w_in, w_ref), (wo_in, wo_ref), (short_in, short_ref), (skip_in, skip_ref),
                (long_in, long_ref), (tok_in, tok_ref), (emb_in, emb_ref), (gain_in, gain_ref),
            ]
        )
    ]

    hello = pltpu.get_barrier_semaphore()
    greeted = 0
    for r in range(1, LINE):
        pl.semaphore_signal(
            hello, inc=1, device_id=(x * LINE + lax.rem(zc + r, LINE), y), device_id_type=MESH
        )
        greeted += 1
    for r in range(1, NX):
        pl.semaphore_signal(hello, inc=1, device_id=at_x(r), device_id_type=MESH)
        pl.semaphore_signal(hello, inc=1, device_id=at_y(r), device_id_type=MESH)
        greeted += 2
    pl.semaphore_signal(hello, inc=1, device_id=after, device_id_type=MESH)
    pl.semaphore_signal(hello, inc=1, device_id=before, device_id_type=MESH)
    greeted += 2

    @pl.when(x != y)
    def _():
        pl.semaphore_signal(hello, inc=1, device_id=(turned, x), device_id_type=MESH)

    for one in inputs:
        one.start()
    for one in inputs:
        one.wait()
    lane32 = lax.broadcasted_iota(jnp.int32, (32, 128), 1) // 32
    for p in range(4):
        chunk = [w_ref[part, :, p * 128 : (p + 1) * 128] for part in range(3)]
        for n in range(4):
            moved = [
                chunk[part] if part == n else pltpu.roll(chunk[part], (part - n) % 4 * 32, 1)
                for part in range(3)
            ]
            wsend[4 * p + n] = jnp.where(
                lane32 == 0, moved[0], jnp.where(lane32 == 1, moved[1], moved[2])
            )
        wosend[p] = wo_ref[:, p * 128 : (p + 1) * 128]
        for part in range(3):
            sf[0, p, part, 0:7, :] = short_ref[part, :, p * 128 : (p + 1) * 128]
            sf[0, p, part, 7:8, :] = skip_ref[:, p * 128 : (p + 1) * 128]
    lf[0] = long_ref[...].astype(F32)
    wl[x, zc] = wsend[zc]
    e4[y] = emb_ref[pl.ds(pl.multiple_of(x * 128, 128), 128), :]

    @pl.when(x == y)
    def _():
        wt[z, c, x] = wosend[...]

    pl.semaphore_wait(hello, greeted + jnp.where(x == y, 0, 1))

    half = pl.ds(pl.multiple_of(64 * c, 64), 64)
    other = pl.ds(pl.multiple_of(64 - 64 * c, 64), 64)
    order = (4, 3, 5, 2, 6, 1, 7, 0)
    for d in order:
        for n in range(NC):
            if d or n:
                to = lax.rem(z + d, NZ) * NC + lax.rem(c + n, NC)
                send(wsend.at[to], wl.at[x, zc], s1_s, s1_r.at[d], (x * LINE + to, y))
    for r in (2, 1, 3):
        send(
            emb_ref.at[pl.ds(pl.multiple_of(x * 128 + 64 * c, 64), 64)],
            e4.at[y, half], e_s.at[0], e_r.at[r - 1], at_y(r),
        )
    send(tok_ref, tprev, tok_s, tok_r, after)
    send(sf.at[0], sf.at[1], fil_s.at[0], fil_r.at[0], at_y(2))
    send(lf.at[0], lf.at[1], fil_s.at[1], fil_r.at[1], at_y(2))

    @pl.when(x != y)
    def _():
        copy(wosend, wt.at[z, c, y], wo_s, wo_r, (turned, x)).start()

    ids = lax.broadcasted_iota(jnp.int32, (128, 512), 1)

    def onehot(begin, column):
        size = column.shape[0]
        oneh[begin : begin + size, :] = jnp.where(
            ids[:size] == jnp.broadcast_to(column, (size, 512)), 1.0, 0.0
        ).astype(BF16)

    names = tok_ref[...].T
    for tile in range(8):
        onehot(144 + tile * 128, names[:, tile : tile + 1])

    above = lax.broadcasted_iota(jnp.int32, (128, 128), 1) >= lax.broadcasted_iota(
        jnp.int32, (128, 128), 0
    )

    def bands(which, begin, end):
        def build(g, carry):
            rows = jnp.broadcast_to(lf[which, pl.ds(g, 1), :], (128, 128))
            moved = pltpu.roll(rows, 0, 1, stride=1, stride_axis=0)
            band[which, g, 0:128, :] = jnp.where(above, 0.0, moved).astype(BF16)
            band[which, g, 128:256, :] = jnp.where(above, moved, 0.0).astype(BF16)
            return carry

        lax.fori_loop(begin, end, build, 0)

    def columns(which):
        for p in range(4):
            taps[which, p] = sf[which, p, 0].T

    columns(0)
    bands(0, 0, 32)

    def unit(q, d):
        return wl.at[lax.rem(x + q, NX), pl.ds(lax.rem(z + NZ - d, NZ) * NC, NC)]

    def line(d):
        got(unit(0, d) if d else wl.at[x, pl.ds(zc, 1)], s1_r.at[d])
        here = unit(0, d)
        for way, q in ((0, 1), (1, 3)):
            send(here, here, s2_s, s2_r.at[way, d], at_x(q))

    def relay(k):
        d = order[-1 - k]
        for way, q in ((0, 1), (1, 3)):
            here = unit(NX - q, d)
            got(here, s2_r.at[way, d])
            if k % 2 == way:
                send(here, here, s2_s, far_r.at[way], at_x(q))

    for k in range(NZ):
        line(order[-1 - k])
    for k in range(NZ - 2):
        relay(k)
    for r in (1, 3, 2):
        here = e4.at[lax.rem(y + NY - r, NY), half]
        got(here, e_r.at[r - 1])
        send(here, here, e_s.at[1], e_r.at[3], mate)
    relay(NZ - 2)
    relay(NZ - 1)
    got(e4.at[pl.ds(0, 3), other], e_r.at[3])

    total = jnp.zeros((128, 1), F32)
    for k in range(NY):
        piece = e4[k].astype(F32)
        total = total + jnp.sum(piece * piece, axis=1, keepdims=True)
    scale = lax.rsqrt(total * (1.0 / 2048) + 1e-06)
    normed = [
        (e4[k].astype(F32) * scale * gain_ref[k]).astype(BF16) for k in range(NY)
    ]
    got(tprev, tok_r)
    names = jnp.where(s == 0, -1, tprev[...]).T
    onehot(0, names[112:128, 6:7])
    onehot(16, names[:, 7:8])

    for way in range(2):
        got(wl.at[lax.rem(x + 2, NX), pl.ds(0, 8)], far_r.at[way])
    table = jnp.zeros((128, 128), F32)
    for k in range(NX):
        table = table + jnp.dot(
            normed[k], wl[k].reshape(512, 128), preferred_element_type=F32
        )
    tt[0, z, c, x] = table.T[0:96].astype(BF16)

    class Gather:
        def __init__(self, buf):
            self.buf = buf

        def ref(self, hop, step):
            return self.buf.at[lax.rem(z - hop * step + NZ, NZ), c]

        def zsend(self, way, step):
            hop = sign if way == 0 else -sign
            here = self.ref(hop, step - 1)
            send(here, here, az_s, az_r.at[way * 4 + step - 1], at_z(hop))

        def dsend(self, step, here):
            send(here, here, ad_s, ad_r.at[step - 1], mate)

        def xsend(self):
            here = self.buf.at[z, c, x]
            for q in range(1, NX):
                send(here, here, ax_s, ax_r, at_x(q))

        def first(self):
            got(self.buf.at[z, c, pl.ds(0, 3)], ax_r)
            self.zsend(0, 1)
            self.zsend(1, 1)
            self.dsend(1, self.ref(0, 0))

        def step(self, i):
            for way in range(2):
                last = 4 if way == 0 else 3
                if i <= last:
                    here = self.ref(sign if way == 0 else -sign, i)
                    got(here, az_r.at[way * 4 + i - 1])
                    if i < last:
                        self.zsend(way, i + 1)
                    self.dsend(i, here)

        def settle(self, i):
            got(self.buf.at[pl.ds(0, (3, 2, 2, 1)[i - 1]), 0], ad_r.at[i - 1])

        def close(self):
            gone(self.buf.at[0, 0, pl.ds(0, 3)], ax_s)
            gone(self.buf.at[pl.ds(0, 7), 0], az_s)
            gone(self.buf.at[:, 0], ad_s)

    class Spread:
        def __init__(self, n, buf):
            self.n, self.buf = n, buf

        def onward(self, way, step):
            hop = sign if way == 0 else -sign
            here = self.buf.at[lax.rem(z - hop * step + NZ, NZ), c, x]
            if step:
                got(here, wz_r.at[self.n, way * 4 + step - 1])
            if step < (4 if way == 0 else 3):
                send(here, here, wz_s.at[self.n], wz_r.at[self.n, way * 4 + step], at_z(hop))
            if step or way == 0:
                arrive = tx_r.at[step] if self.n == 0 else wx_r
                for q in (2, 1, 3):
                    send(here, here, wx_s.at[self.n], arrive, at_x(q))

        def step(self, i):
            self.onward(0, i)
            if i < 4:
                self.onward(1, i)

        def across(self, i):
            hops = ((0,), (sign, -sign), (sign, -sign), (sign, -sign), (sign,))[i]
            got(self.buf.at[pl.ds(0, len(hops)), 0, pl.ds(0, 3)], tx_r.at[i])
            for hop in hops:
                here = self.buf.at[lax.rem(z - hop * i + NZ, NZ), c]
                send(here, here, wd_s.at[0], td_r.at[max(i, 1) - 1], mate)

        def settle(self, i):
            got(self.buf.at[pl.ds(0, (3, 2, 2, 1)[i - 1]), 0], td_r.at[i - 1])

        def share(self):
            got(self.buf.at[pl.ds(0, 3)], wx_r)
            here = self.buf.at[:, c]
            send(here, here, wd_s.at[1], wd_r, mate)

        def shared(self):
            got(self.buf.at[:, 1 - c], wd_r)

        def close(self):
            gone(self.buf.at[pl.ds(0, 7), 0, 0], wz_s.at[self.n])
            gone(self.buf.at[pl.ds(0, 3)], wx_s.at[self.n])
            gone(self.buf.at[:, c], wd_s.at[self.n])

    table_own = Spread(0, tt.at[0])
    table_far = Gather(tt.at[1])
    outw = Spread(1, wt)

    table_own.step(0)
    send(tt.at[0, z, c, x], tt.at[1, z, c, x], t2_s, t2_r, at_y(2))
    got(sf.at[1], fil_r.at[0])
    got(lf.at[1], fil_r.at[1])
    columns(1)
    bands(1, 0, 16)
    table_own.step(1)
    bands(1, 16, 24)
    table_own.step(2)
    bands(1, 24, 32)
    got(tt.at[1, z, c, x], t2_r)
    table_far.xsend()

    @pl.when(x != y)
    def _():
        copy(wosend, wt.at[z, c, x], wo_s, wo_r, mate).wait()

    table_own.across(0)
    table_own.across(1)

    pair0 = z // 2
    even = 1 - 2 * lax.rem(z, 2)

    def pair(i):
        move = (0, -even, even, 2)[i - 1]
        return lax.rem(pair0 + move + 4, 4)

    def block(which, k, p, early=None, late=None):
        table = jnp.concatenate(
            [
                jnp.concatenate(
                    [
                        tt[which, 2 * p + n // 2, n % 2, b, part * 32 : (part + 1) * 32, :]
                        for part in range(3)
                        for n in range(4)
                    ],
                    axis=0,
                )
                for b in range(NX)
            ],
            axis=1,
        )
        tabn[...] = table.T
        for begin, end in ((0, 304), (304, 592), (592, 880), (880, 1168)):
            rows = slice(begin, end)
            both = jnp.dot(oneh[rows, :], tabn[...], preferred_element_type=F32)
            for part in range(3):
                proj[part, rows, :] = both[:, part * 128 : (part + 1) * 128]

        if early:
            early()

        def fir(part, row, count):
            total = None
            for lag in range(7):
                tap = jnp.broadcast_to(sf[which, p, part, lag : lag + 1, :], (count, 128))
                term = tap * proj[part, pl.ds(row - lag, count), :]
                total = term if total is None else total + term
            return total

        def tile(n, query):
            row = pl.multiple_of(n * 128 + 16, 16)
            pieces = [
                (fir(1, row + 32 * h, 32) * fir(2, row + 32 * h, 32)).astype(BF16) for h in range(4)
            ]
            pt[n] = jnp.concatenate(pieces, axis=0).T
            if query:
                pieces = [fir(0, row + 32 * h, 32).astype(BF16) for h in range(4)]
                qt[n] = jnp.concatenate(pieces, axis=0).T

        def tiles(n, carry):
            tile(n, True)
            return carry

        tile(0, False)
        lax.fori_loop(1, 9, tiles, 0)
        if late:
            late()

        def groups(h, carry):
            for n in range(4):
                g = 4 * h + n
                ch = pl.ds(pl.multiple_of(g * 16, 16), 16)
                prod = [pt[t, ch, :] for t in range(9)]
                rows = jnp.concatenate(
                    [jnp.concatenate([prod[t], prod[t + 1]], axis=1) for t in range(8)], axis=0
                )
                conv = jnp.dot(rows, band[which, 8 * p + g], preferred_element_type=F32).astype(BF16)
                skip = jnp.broadcast_to(taps[which, p, ch, 7:8], (16, 128)).astype(BF16)
                for t in range(8):
                    whole = conv[t * 16 : (t + 1) * 16] + skip * prod[t + 1]
                    g4[k, p, ch, t * 128 : (t + 1) * 128] = qt[t + 1, ch, :] * whole
            return carry

        lax.fori_loop(0, 2, groups, 0)

    def gsend(i):
        here = g4.at[y, pair(i)]
        for way, q in ((0, 1), (1, 3)):
            send(here, here, g_s, g_r.at[way], at_y(q))

    def own(i, **hooks):
        table_own.settle(i)
        block(0, y, pair(i), **hooks)
        gsend(i)

    def others(i, **hooks):
        table_far.settle(i)
        block(1, far, pair(i), **hooks)

    def resid():
        below = lax.broadcasted_iota(jnp.int32, (512, 128), 0)
        for n in range(8):
            row = tok_ref[n : n + 1, :]
            onet[:, n * 128 : (n + 1) * 128] = jnp.where(below == row, 1.0, 0.0).astype(BF16)
        for n in range(4):
            cols = slice(n * 128, (n + 1) * 128)
            acc[cols, :] = jnp.dot(emb_ref[:, cols].T, onet[...], preferred_element_type=F32)

    def late1():
        table_own.step(3)
        table_own.across(2)
        table_far.first()

    def early2():
        table_own.step(4)
        table_own.across(3)
        outw.step(0)

    def early3():
        table_own.across(4)
        outw.step(1)

    def late4():
        resid()
        table_far.step(3)

    own(1, late=late1)
    own(2, early=early2, late=lambda: table_far.step(1))
    own(3, early=early3, late=lambda: table_far.step(2))
    own(4, early=lambda: outw.step(2), late=late4)
    others(1, early=lambda: outw.step(3), late=lambda: table_far.step(4))
    others(2, early=lambda: outw.step(4))
    others(3)
    others(4, early=outw.share)
    outw.shared()

    def project(ks, n):
        sums = None
        for k in ks:
            left = jnp.concatenate(
                [wt[pl.ds(2 * n, 2), :, k, p].reshape(128, 128) for p in range(4)], axis=1
            )
            term = jnp.dot(left, g4[k].reshape(512, 1024), preferred_element_type=F32)
            sums = term if sums is None else sums + term
        return sums

    def near(n, carry):
        cols = pl.ds(pl.multiple_of(n * 128, 128), 128)
        acc[cols, :] = acc[cols, :] + project((y, far), n)
        return carry

    lax.fori_loop(0, 4, near, 0)
    for way, q in ((0, 3), (1, 1)):
        got(g4.at[lax.rem(y + q, NY)], g_r.at[way])

    def rest(n, carry):
        rows = pl.ds(pl.multiple_of(n * 128, 128), 128)
        ks = (lax.rem(y + 1, NY), lax.rem(y + 3, NY))
        stage[rows, :] = (acc[rows, :] + project(ks, n)).astype(BF16)
        pltpu.make_async_copy(stage.at[rows], out_ref.at[rows], out_s).start()
        return carry

    lax.fori_loop(0, 4, rest, 0)
    gone(wsend.at[pl.ds(0, LINE - 1)], s1_s)
    gone(wl.at[pl.ds(0, 3)], s2_s)
    for n in range(2):
        gone(e4.at[pl.ds(0, 3), half], e_s.at[n])
        gone((sf, lf)[n].at[0], fil_s.at[n])
    gone(tok_ref, tok_s)
    gone(tt.at[0, z, c, x], t2_s)
    gone(g4.at[pl.ds(0, 2)], g_s)
    for one in (table_own, table_far, outw):
        one.close()
    pltpu.make_async_copy(stage, out_ref, out_s).wait()


def body(
    token_ids, embed_table, norm_gain, in_weight, short_filter, long_filter, long_skip, out_weight
):
    tok = token_ids.reshape(8, 128)
    gain = norm_gain.reshape(4, 1, 512)
    w = in_weight.transpose(1, 0, 2)
    short = short_filter.transpose(1, 0, 2)
    skip = long_skip.reshape(1, 512)
    dma = pltpu.SemaphoreType.DMA
    out = pl.pallas_call(
        kernel,
        out_shape=jax.ShapeDtypeStruct((512, 1024), BF16),
        in_specs=[pl.BlockSpec(memory_space=pl.ANY)] * 8,
        out_specs=pl.BlockSpec(memory_space=pl.ANY),
        scratch_shapes=[
            pltpu.VMEM((8, 128), jnp.int32),
            pltpu.VMEM((512, 512), BF16),
            pltpu.VMEM((4, 1, 512), F32),
            pltpu.VMEM((3, 32, 512), BF16),
            pltpu.VMEM((32, 512), BF16),
            pltpu.VMEM((3, 7, 512), F32),
            pltpu.VMEM((1, 512), F32),
            pltpu.VMEM((32, 128), BF16),
            dma((8,)),
            pltpu.VMEM((8, 128), jnp.int32),
            pltpu.VMEM((2, 4, 3, 8, 128), F32),
            pltpu.VMEM((2, 32, 128), F32),
            pltpu.VMEM((LINE, 32, 128), BF16),
            pltpu.VMEM((4, 32, 128), BF16),
            pltpu.VMEM((NX, LINE, 32, 128), BF16),
            pltpu.VMEM((NY, 128, 512), BF16),
            pltpu.VMEM((2, NZ, NC, NX, 96, 128), BF16),
            pltpu.VMEM((NZ, NC, NX, 4, 32, 128), BF16),
            pltpu.VMEM((NY, 4, 128, 1024), BF16),
            pltpu.VMEM((ROWS, 512), BF16),
            pltpu.VMEM((2, 32, 256, 128), BF16),
            pltpu.VMEM((2, 4, 128, 8), F32),
            pltpu.VMEM((512, 384), BF16),
            pltpu.VMEM((3, ROWS, 128), F32),
            pltpu.VMEM((9, 128, 128), BF16),
            pltpu.VMEM((9, 128, 128), BF16),
            pltpu.VMEM((512, 1024), BF16),
            pltpu.VMEM((512, 1024), F32),
            pltpu.VMEM((512, 1024), BF16),
            dma, dma, dma((2,)), dma((2,)), dma, dma((8,)), dma, dma((2, 8)), dma((2,)),
            dma((2,)), dma((4,)), dma, dma, dma, dma,
            dma, dma, dma, dma((8,)), dma, dma((4,)),
            dma((2,)), dma((2, 8)), dma((2,)), dma, dma((2,)), dma, dma((5,)), dma((4,)),
            dma, dma((2,)), dma,
        ],
        compiler_params=pltpu.CompilerParams(
            collective_id=0, has_side_effects=True, vmem_limit_bytes=60 * 2**20
        ),
    )(tok, embed_table, gain, w, out_weight.T, short, skip, long_filter)
    return out.T


def solution(mesh):
    placed = (
        P("seq"),
        P(None, "tp"),
        P(),
        P("seq", None, "tp"),
        P(None, None, "tp"),
        P("tp", None),
        P("tp"),
        P("tp", "seq"),
    )
    return jax.shard_map(
        body, mesh=mesh, in_specs=placed, out_specs=P("seq", "tp"), check_vma=False
    )
```
